32 devices in a mesh: branch: 4 (over z), seq: 2 (over x), rep: 4 (over y, core).
Axes of the slice: x: 2, y: 2, z: 4, core: 2. Of those that a mesh axis runs over, the one named last changes fastest.
Arguments:
- noisy: bfloat16 [4, 1024, 5120], P('rep'), may hold values from -6 to 6
- generated: bfloat16 [4, 1024, 5120], P('rep', 'seq'), may hold values from -170 to 170
- caption: bfloat16 [4, 5120], P('rep'), may hold values from -0.59765625 to 0.59765625
- null_caption: bfloat16 [5120], replicated, may hold values from -0.59765625 to 0.59765625
- caption_drop: int32 [4], P('rep'), may hold values from 0 to 1, as said below
- timestep: int32 [4], P('rep'), may hold values from 0 to 999
- window_start: int32 [4], P('rep'), may hold values from 0 to 31736
- teacher_qkv: bfloat16 [3, 5120, 1024], P(None, None, ('branch', 'seq')), may hold values from -0.078125 to 0.078125
- teacher_out: bfloat16 [1024, 5120], P(('branch', 'seq')), may hold values from -0.1875 to 0.1875
- teacher_gain: float32 [5120], replicated, may hold values from 0.5 to 1.5
- teacher_qk_gain: float32 [2, 1024], P(None, ('branch', 'seq')), may hold values from 0.7 to 2.6
- critic_qkv: bfloat16 [3, 5120, 1024], P(None, None, ('branch', 'seq')), may hold values from -0.078125 to 0.078125
- critic_out: bfloat16 [1024, 5120], P(('branch', 'seq')), may hold values from -0.1875 to 0.1875
- critic_gain: float32 [5120], replicated, may hold values from 0.5 to 1.5
- critic_qk_gain: float32 [2, 1024], P(None, ('branch', 'seq')), may hold values from 0.7 to 2.6
Outputs:
- generator_grad: bfloat16 [4, 1024, 5120], P('rep', 'seq')
- critic_qkv_grad: float32 [3, 5120, 1024], P(None, 'rep', ('branch', 'seq'))
- critic_out_grad: float32 [1024, 5120], P(('branch', 'seq'), 'rep')
The draws below stay inside these ranges and needn't reach their ends.
Inputs may be any that keep to these rules, and one draw needn't show every extreme that they name: `caption_drop`: each window's flag is drawn independently.
All inputs are finite; a program needn't handle non-finite values. Where the reference program divides by a largest or mean magnitude, that divisor is 1e-20 or more.
Results may differ from the reference program's by a relative error of at most 0.018.
The reference program's roundings to bfloat16 on the way count: a program that leaves them out, or rounds other values in their place, can miss the bound.
Values may be sent and summed in bfloat16 or wider, within the bound.
No kernel may reach another device: no remote copies, remote signals or barrier semaphores. Data moves between devices by JAX's collectives and lax.ppermute only.
A program may use at most 192 MiB of HBM per device.

```python
import math
import jax
import jax.numpy as jnp
from jax import lax

D = 5120
HEAD = 128
HEADS_DEV = 1
LEN = 1024
FRAMES = 21
GRID_H = 30
GRID_W = 52
H = 8
HT = 1024
SAMPLES = 4


def draw_generated(key, part):
    base_key = jax.random.fold_in(key, 11)
    key_list = jax.random.split(base_key, 3)
    base = jnp.clip(jax.random.normal(key_list[0], (SAMPLES, LEN, D), jnp.float32), -5.0, 5.0)
    rising = jnp.exp(jnp.log(3.0) * jnp.arange(LEN, dtype=jnp.float32) / (LEN - 1.0))
    row_scale = jnp.exp(jax.random.uniform(key_list[1], (SAMPLES, LEN, 1), jnp.float32, 0.0, jnp.log(10.0)))
    column_scale = jnp.exp(jax.random.uniform(key_list[2], (1, 1, D), jnp.float32, 0.0, jnp.log(10.0)))
    return (base * row_scale * column_scale * rising[None, :, None] / 16.0).astype(jnp.bfloat16)


def draw_caption_drop(key, part):
    drop_key = jax.random.fold_in(key, 23)
    return jax.random.randint(drop_key, (SAMPLES,), 0, 2, jnp.int32)


def place_ends(array, rng, least, high):
    shape = array.shape
    spot = [jax.random.randint(jax.random.fold_in(rng, axis), (), 0, shape[axis]) for axis in range(len(shape))]
    array = array.at[tuple(spot)].set(least)
    longest = shape.index(max(shape))
    spot[longest] = (spot[longest] + 1) % shape[longest]
    return array.at[tuple(spot)].set(high)


def steps_of(own_key, dims, cuts, low, largest):
    def one(position, blocks):
        heights = jax.random.uniform(jax.random.fold_in(jax.random.fold_in(own_key, 6), position), (blocks,), jnp.float32, low / len(cuts), largest / len(cuts))
        return jnp.repeat(jnp.exp(heights), dims[position] // blocks).reshape((-1,) + (1,) * (len(dims) - position - 1))

    gain = one(*cuts[0])
    for cut in cuts[1:]:
        gain = gain * one(*cut)
    return gain


def scatter_about(stream_key, shape, width, reach, shards=(), held_as=jnp.bfloat16):
    result = jax.random.normal(stream_key, shape, jnp.float32) * width
    if len(shards) > 0:
        result = steps_of(stream_key, shape, shards, -0.22, 0.18) * result
    return jnp.clip(result, min=-reach, max=reach).astype(held_as)


def setup_inputs(seed: int = 0) -> dict:
    streams_of = jax.random.split(jax.random.key(seed), 16)
    return {
        "noisy": scatter_about(streams_of[0], (SAMPLES, LEN, D), 1.0, 6.0, ((0, 4),)),
        "generated": draw_generated(jax.random.fold_in(streams_of[15], 71), 0),
        "caption": scatter_about(streams_of[2], (SAMPLES, D), 0.1, 0.59765625, ((0, 4),)),
        "null_caption": scatter_about(streams_of[3], (D,), 0.1, 0.59765625),
        "caption_drop": draw_caption_drop(jax.random.fold_in(streams_of[15], 71), 0),
        "timestep": place_ends(jax.random.randint(streams_of[5], (SAMPLES,), 0, 1000), jax.random.fold_in(streams_of[5], 1), 0, 999).astype(jnp.int32),
        "window_start": place_ends(jax.random.randint(streams_of[6], (SAMPLES,), 0, FRAMES * GRID_H * GRID_W - LEN + 1), jax.random.fold_in(streams_of[6], 1), 0, FRAMES * GRID_H * GRID_W - LEN).astype(jnp.int32),
        "teacher_qkv": scatter_about(streams_of[7], (3, D, HT), D ** -0.5, 0.078125, ((2, 8),)),
        "teacher_out": scatter_about(streams_of[8], (HT, D), HT ** -0.5, 0.1875, ((0, 8),)),
        "teacher_gain": jnp.clip(1.0 + 0.1 * jax.random.normal(streams_of[9], (D,), jnp.float32), 0.5, 1.5),
        "teacher_qk_gain": jnp.clip(jnp.exp(math.log(2.6) - 1.3121864 * jax.random.uniform(streams_of[10], (2, HT), jnp.float32) ** steps_of(streams_of[10], (2, HT), ((1, 8),), -0.2, 0.2)), 0.7, 2.6),
        "critic_qkv": scatter_about(streams_of[11], (3, D, HT), D ** -0.5, 0.078125, ((2, 8),)),
        "critic_out": scatter_about(streams_of[12], (HT, D), HT ** -0.5, 0.1875, ((0, 8),)),
        "critic_gain": jnp.clip(1.0 + 0.1 * jax.random.normal(streams_of[13], (D,), jnp.float32), 0.5, 1.5),
        "critic_qk_gain": jnp.clip(jnp.exp(math.log(2.6) - 1.3121864 * jax.random.uniform(streams_of[14], (2, HT), jnp.float32) ** steps_of(streams_of[14], (2, HT), ((1, 8),), -0.2, 0.2)), 0.7, 2.6),
    }


guidance = 5.0
score_scale = 128.0 ** (-0.5)
norm_eps = 1e-06

def rounded(values):
    return lax.optimization_barrier(values.astype(jnp.bfloat16))

def rope_tables(first_token):
    token_index = first_token + jnp.arange(LEN, dtype=jnp.int32)
    plane_size = GRID_H * GRID_W
    frame_index = token_index // plane_size
    remainder = token_index - frame_index * plane_size
    row_index = remainder // GRID_W
    column_index = remainder - row_index * GRID_W
    pair_index = jnp.arange(64, dtype=jnp.int32)
    in_frames = pair_index < 22
    in_rows = jnp.logical_and(pair_index >= 22, pair_index < 43)
    local_rank = jnp.where(in_frames, pair_index, jnp.where(in_rows, pair_index - 22, pair_index - 43)).astype(jnp.float32)
    axis_width = jnp.where(in_frames, 44.0, 42.0).astype(jnp.float32)
    frequency = jnp.exp(-jnp.log(10000.0) * 2.0 * local_rank / axis_width)
    chosen = jnp.where(in_frames[None, :], frame_index[:, None], jnp.where(in_rows[None, :], row_index[:, None], column_index[:, None])).astype(jnp.float32)
    angles = chosen * frequency[None, :]
    angles = jnp.concatenate([angles, angles], axis=1)
    return (jnp.cos(angles), jnp.sin(angles))

def rotate_half(values):
    return jnp.concatenate([-values[..., 64:], values[..., :64]], axis=-1)

def rotate_back(values):
    return jnp.concatenate([values[..., 64:], -values[..., :64]], axis=-1)

def norm_tokens(inputs, gain_values):
    scaled = inputs * lax.rsqrt(lax.optimization_barrier(jnp.mean(inputs * inputs, axis=-1, keepdims=True)) + norm_eps) * gain_values
    return rounded(scaled)

def undo_norm(raw_values, inverse, gain_values, grad_normed):
    scaled = gain_values * grad_normed
    return inverse * scaled - raw_values * inverse * inverse * inverse * lax.optimization_barrier(jnp.mean(scaled * raw_values, axis=-1, keepdims=True))

def head_forward(hidden, weights, qk_gains, cosine_table, sine_table):
    projected = jnp.einsum('sd,kdc->ksc', hidden.astype(jnp.float32), weights.astype(jnp.float32))
    length = hidden.shape[0]
    query_raw = projected[0].reshape(length, -1, 128)
    key_raw = projected[1].reshape(length, -1, 128)
    value_rows = rounded(projected[2].reshape(length, -1, 128))
    gain_query = qk_gains[0].reshape(-1, 128)
    gain_key = qk_gains[1].reshape(-1, 128)
    inv_query = lax.rsqrt(lax.optimization_barrier(jnp.mean(query_raw * query_raw, axis=-1, keepdims=True)) + norm_eps)
    inv_key = lax.rsqrt(lax.optimization_barrier(jnp.mean(key_raw * key_raw, axis=-1, keepdims=True)) + norm_eps)
    normed_query = query_raw * inv_query * gain_query
    normed_key = key_raw * inv_key * gain_key
    cosine_h = cosine_table[:, None, :]
    sine_h = sine_table[:, None, :]
    rope_query = rounded(normed_query * cosine_h + rotate_half(normed_query) * sine_h)
    rope_key = rounded(normed_key * cosine_h + rotate_half(normed_key) * sine_h)
    scores = jnp.einsum('qhe,khe->hqk', rope_query.astype(jnp.float32), rope_key.astype(jnp.float32)) * score_scale
    exponent = jnp.exp(scores)
    probability = exponent / lax.optimization_barrier(jnp.sum(exponent, axis=-1, keepdims=True))
    prob_rounded = rounded(probability)
    attended = jnp.einsum('hqk,khe->qhe', prob_rounded.astype(jnp.float32), value_rows.astype(jnp.float32))
    attended = rounded(attended).reshape(length, -1)
    saved_state = (query_raw, key_raw, inv_query, inv_key, rope_query, rope_key, value_rows, probability, prob_rounded)
    return (attended, saved_state)

def head_backward(hidden, grad_attn, saved_state, qk_gains, cosine_table, sine_table):
    query_raw, key_raw, inv_query, inv_key, rope_query, rope_key, value_rows, probability, prob_rounded = saved_state
    length = hidden.shape[0]
    grad_heads = grad_attn.reshape(length, -1, 128).astype(jnp.float32)
    grad_prob = jnp.einsum('qhe,khe->hqk', grad_heads, value_rows.astype(jnp.float32))
    grad_score = probability * (grad_prob - lax.optimization_barrier(jnp.sum(grad_prob * probability, axis=-1, keepdims=True))) * score_scale
    grad_score = rounded(grad_score).astype(jnp.float32)
    grad_qrot = jnp.einsum('hqk,khe->qhe', grad_score, rope_key.astype(jnp.float32))
    grad_krot = jnp.einsum('hqk,qhe->khe', grad_score, rope_query.astype(jnp.float32))
    grad_value = jnp.einsum('hqk,qhe->khe', prob_rounded.astype(jnp.float32), grad_heads)
    cosine_h = cosine_table[:, None, :]
    sine_h = sine_table[:, None, :]
    grad_qnorm = grad_qrot * cosine_h + rotate_back(grad_qrot * sine_h)
    grad_knorm = grad_krot * cosine_h + rotate_back(grad_krot * sine_h)
    grad_query = undo_norm(query_raw, inv_query, qk_gains[0].reshape(-1, 128), grad_qnorm)
    grad_key = undo_norm(key_raw, inv_key, qk_gains[1].reshape(-1, 128), grad_knorm)
    grad_stack = rounded(jnp.stack([grad_query.reshape(length, -1), grad_key.reshape(length, -1), grad_value.reshape(length, -1)]))
    return jnp.einsum('sd,ksc->kdc', hidden.astype(jnp.float32), grad_stack.astype(jnp.float32))

def reference(noisy, generated, caption, null_caption, caption_drop, timestep, window_start, teacher_qkv, teacher_out, teacher_gain, teacher_qk_gain, critic_qkv, critic_out, critic_gain, critic_qk_gain):
    group_width = HEAD * HEADS_DEV
    group_total = H // HEADS_DEV
    group_ids = jnp.arange(group_total, dtype=jnp.int32)

    def one_sample(totals, sample_data):
        latent_row, target_row, caption_row, drop_flag, step_index, first_token = sample_data
        fraction = (step_index.astype(jnp.float32) + 1.0) / 1001.0
        noise_level = 5.0 * fraction / (1.0 + 4.0 * fraction)
        used_caption = jnp.where(drop_flag == 1, null_caption, caption_row)
        latent = latent_row.astype(jnp.float32)
        cond_input = latent + used_caption.astype(jnp.float32)[None, :]
        null_input = latent + null_caption.astype(jnp.float32)[None, :]
        cond_normed = norm_tokens(cond_input, teacher_gain)
        null_normed = norm_tokens(null_input, teacher_gain)
        critic_normed = norm_tokens(cond_input, critic_gain)
        cosine_table, sine_table = rope_tables(first_token)

        def slices(group_id):
            first_col = (group_id * group_width).astype(jnp.int32)
            return (lax.dynamic_slice_in_dim(teacher_qkv, first_col, group_width, 2), lax.dynamic_slice_in_dim(teacher_qk_gain, first_col, group_width, 1), lax.dynamic_slice_in_dim(teacher_out, first_col, group_width, 0), lax.dynamic_slice_in_dim(critic_qkv, first_col, group_width, 2), lax.dynamic_slice_in_dim(critic_qk_gain, first_col, group_width, 1), lax.dynamic_slice_in_dim(critic_out, first_col, group_width, 0))

        def forward_group(running, group_id):
            teacher_cols, teacher_gains, teacher_rows, critic_cols, critic_gains, critic_rows = slices(group_id)
            cond_attn, unused = head_forward(cond_normed, teacher_cols, teacher_gains, cosine_table, sine_table)
            null_attn, unused = head_forward(null_normed, teacher_cols, teacher_gains, cosine_table, sine_table)
            fake_attn, unused = head_forward(critic_normed, critic_cols, critic_gains, cosine_table, sine_table)
            cond_part = jnp.dot(cond_attn, teacher_rows, preferred_element_type=jnp.float32)
            null_part = jnp.dot(null_attn, teacher_rows, preferred_element_type=jnp.float32)
            fake_part = jnp.dot(fake_attn, critic_rows, preferred_element_type=jnp.float32)
            guided_term = rounded(guidance * cond_part - (guidance - 1.0) * null_part).astype(jnp.float32)
            fake_term = rounded(fake_part).astype(jnp.float32)
            return ((running[0] + guided_term, running[1] + fake_term), None)
        empty_sum = jnp.zeros((LEN, D), jnp.float32)
        (guided_sum, fake_sum), unused = lax.scan(forward_group, (empty_sum, empty_sum), group_ids)
        real_velocity = guidance * cond_input - (guidance - 1.0) * null_input + guided_sum
        fake_velocity = cond_input + fake_sum
        real_pred = latent - noise_level * real_velocity
        fake_pred = latent - noise_level * fake_velocity
        target = target_row.astype(jnp.float32)
        spread = jnp.mean(jnp.abs(real_pred - target))
        generator_grad = ((fake_pred - real_pred) / (spread + 1e-05)).astype(jnp.bfloat16)
        fake_cotangent = rounded(-noise_level * (fake_pred - target) / 64.0)

        def backward_group(carried, group_id):
            teacher_cols, teacher_gains, teacher_rows, critic_cols, critic_gains, critic_rows = slices(group_id)
            fake_attn, saved_state = head_forward(critic_normed, critic_cols, critic_gains, cosine_table, sine_table)
            out_part = jnp.dot(fake_attn.T, fake_cotangent, preferred_element_type=jnp.float32)
            grad_attn = rounded(jnp.dot(fake_cotangent, critic_rows.T, preferred_element_type=jnp.float32))
            proj_part = head_backward(critic_normed, grad_attn, saved_state, critic_gains, cosine_table, sine_table)
            return (carried, (proj_part, out_part))
        carried, (proj_parts, out_parts) = lax.scan(backward_group, jnp.zeros((), jnp.float32), group_ids)
        proj_grads = jnp.transpose(proj_parts, (1, 2, 0, 3)).reshape(3, D, HT)
        out_grads = out_parts.reshape(HT, D)
        return ((totals[0] + proj_grads, totals[1] + out_grads), generator_grad)
    start_totals = (jnp.zeros((3, D, HT), jnp.float32), jnp.zeros((HT, D), jnp.float32))
    (proj_total, out_total), generator_grad = lax.scan(one_sample, start_totals, (noisy, generated, caption, caption_drop, timestep, window_start))
    return (generator_grad, proj_total, out_total)
```

```python
import functools
import jax
import jax.numpy as jnp
from jax import lax
from jax.experimental import pallas as pl
from jax.experimental.pallas import tpu as pltpu
from jax.sharding import PartitionSpec as P

GRID_H = 30
GRID_W = 52

guidance = 5.0
norm_eps = 1e-06

ANY = pl.BlockSpec(memory_space=pl.ANY)
SMEM = pl.BlockSpec(memory_space=pltpu.SMEM)
F32, BF16 = jnp.float32, jnp.bfloat16


def swap(size, bit):
    return [(i, i ^ bit) for i in range(size)]


def bits_of(size):
    return [1 << k for k in range(size.bit_length() - 1)]


def move(value, axis, bit):
    return lax.ppermute(value, axis, swap(lax.axis_size(axis), bit))


def rope_tables(first_token, length):
    token_index = first_token + jnp.arange(length, dtype=jnp.int32)
    plane_size = GRID_H * GRID_W
    frame_index = token_index // plane_size
    remainder = token_index - frame_index * plane_size
    row_index = remainder // GRID_W
    column_index = remainder - row_index * GRID_W
    pair_index = jnp.arange(64, dtype=jnp.int32)
    in_frames = pair_index < 22
    in_rows = jnp.logical_and(pair_index >= 22, pair_index < 43)
    local_rank = jnp.where(
        in_frames, pair_index, jnp.where(in_rows, pair_index - 22, pair_index - 43)
    ).astype(jnp.float32)
    axis_width = jnp.where(in_frames, 44.0, 42.0).astype(jnp.float32)
    frequency = jnp.exp(-jnp.log(10000.0) * 2.0 * local_rank / axis_width)
    chosen = jnp.where(
        in_frames[None, :],
        frame_index[:, None],
        jnp.where(in_rows[None, :], row_index[:, None], column_index[:, None]),
    ).astype(jnp.float32)
    angles = chosen * frequency[None, :]
    angles = jnp.concatenate([angles, angles], axis=1)
    return (jnp.cos(angles), jnp.sin(angles))


def dot(left, right):
    return jnp.dot(left, right, preferred_element_type=F32)


def contract(left, right, left_dim, right_dim):
    return lax.dot_general(
        left, right, (((left_dim,), (right_dim,)), ((), ())), preferred_element_type=F32
    )


def rotate_half(values):
    half = values.shape[-1] // 2
    return jnp.concatenate([-values[..., half:], values[..., :half]], axis=-1)


def rotate_back(values):
    half = values.shape[-1] // 2
    return jnp.concatenate([values[..., half:], -values[..., :half]], axis=-1)


def resident(shape):
    return pl.BlockSpec(shape, lambda *_: (0,) * len(shape), pipeline_mode=pl.Buffered(1))


def project_kernel(variants, keep, held, noisy_ref, shift_ref, gain_ref, weight_ref, *refs):
    refs = refs[held:]
    out_ref = refs[0]
    hidden_ref = refs[1] if keep else None
    joined, normed = refs[-2:]
    tile, width = noisy_ref.shape
    head = weight_ref.shape[2]

    @pl.when(pl.program_id(0) == 0)
    def _():
        for k in range(3):
            joined[:, k * head : (k + 1) * head] = weight_ref[k]

    def step(t, carry):
        at = pl.ds(pl.multiple_of(t * 16, 16), 16)
        latent = noisy_ref[at, :].astype(F32)
        for v in range(variants):
            shifted = latent + shift_ref[v : v + 1, :]
            mean = jnp.sum(shifted * shifted, axis=-1, keepdims=True) / width
            scaled = shifted * lax.rsqrt(mean + norm_eps) * gain_ref[...]
            normed[v, at, :] = scaled.astype(BF16)
        return carry

    lax.fori_loop(0, tile // 16, step, 0)
    for v in range(variants):
        out_ref[v] = dot(normed[v], joined[...])
    if keep:
        hidden_ref[...] = normed[0]


def project(noisy, shifts, gain, weight, keep, start, count, into=()):
    length, width = noisy.shape
    head = weight.shape[2]
    variants = shifts.shape[0]
    tile = min(256, count)
    first = start // tile
    out_shape = [jax.ShapeDtypeStruct((variants, length, 3 * head), F32)]
    out_specs = [pl.BlockSpec((variants, tile, 3 * head), lambda i: (0, first + i, 0))]
    if keep:
        out_shape.append(jax.ShapeDtypeStruct((length, width), BF16))
        out_specs.append(pl.BlockSpec((tile, width), lambda i: (first + i, 0)))
    return pl.pallas_call(
        functools.partial(project_kernel, variants, keep, len(into)),
        grid=(count // tile,),
        in_specs=[
            pl.BlockSpec((tile, width), lambda i: (first + i, 0)),
            resident((variants, width)),
            resident((1, width)),
            resident(weight.shape),
        ]
        + [ANY] * len(into),
        out_specs=out_specs,
        out_shape=out_shape,
        input_output_aliases={4 + n: n for n in range(len(into))},
        scratch_shapes=[
            pltpu.VMEM((width, 3 * head), BF16),
            pltpu.VMEM((variants, tile, width), BF16),
        ],
        cost_estimate=pl.CostEstimate(
            flops=2 * variants * count * width * 3 * head,
            bytes_accessed=2 * count * width * (2 if keep else 1) + 6 * width * head,
            transcendentals=0,
        ),
    )(noisy, shifts, gain, weight, *into)


def rope_rows(raw, gain, cosine, sine):
    inverse = lax.rsqrt(jnp.mean(raw * raw, axis=-1, keepdims=True) + norm_eps)
    normed = raw * inverse * gain
    return (normed * cosine + rotate_half(normed) * sine).astype(BF16)


def softmax_rows(query, key, scale):
    exponent = jnp.exp(contract(query, key, 1, 1) * scale)
    return exponent / jnp.sum(exponent, axis=-1, keepdims=True)


def attend_kernel(variants, qkv_ref, gain_ref, cos_ref, sin_ref, out_ref, *refs):
    keys, values = refs[-2:]
    saves = refs[:-2]
    head = out_ref.shape[1]
    tile = out_ref.shape[0]
    scale = head ** (-0.5)
    i = pl.program_id(0)

    @pl.when(i == 0)
    def _():
        for v in range(variants):
            keys[v] = rope_rows(
                qkv_ref[v, :, head : 2 * head], gain_ref[1:2, :], cos_ref[...], sin_ref[...]
            )
            values[v] = qkv_ref[v, :, 2 * head :].astype(BF16)
        if saves:
            saves[1][...] = keys[0]
            saves[2][...] = values[0]

    at = pl.ds(pl.multiple_of(i * tile, tile), tile)
    results = []
    for v in range(variants):
        query = rope_rows(qkv_ref[v, at, :head], gain_ref[0:1, :], cos_ref[at, :], sin_ref[at, :])
        if saves:
            saves[0][...] = query
        prob = softmax_rows(query, keys[v], scale).astype(BF16)
        results.append(dot(prob, values[v]).astype(BF16))
    if variants == 1:
        out_ref[...] = results[0]
    else:
        guided = guidance * results[0].astype(F32) - (guidance - 1.0) * results[1].astype(F32)
        out_ref[...] = guided.astype(BF16)


def attend(qkv, gains, cosine, sine, keep):
    variants, length, triple = qkv.shape
    head = triple // 3
    tile = min(256, length)
    count = 4 if keep else 1
    row = pl.BlockSpec((tile, head), lambda i: (i, 0))
    whole = pl.BlockSpec((length, head), lambda i: (0, 0))
    return pl.pallas_call(
        functools.partial(attend_kernel, variants),
        grid=(length // tile,),
        in_specs=[
            resident(qkv.shape),
            resident(gains.shape),
            resident(cosine.shape),
            resident(sine.shape),
        ],
        out_specs=[row, row, whole, whole][:count],
        out_shape=[jax.ShapeDtypeStruct((length, head), BF16)] * count,
        scratch_shapes=[
            pltpu.VMEM((variants, length, head), BF16),
            pltpu.VMEM((variants, length, head), BF16),
        ],
        cost_estimate=pl.CostEstimate(
            flops=16 * variants * length * length * head,
            bytes_accessed=4 * variants * length * triple,
            transcendentals=variants * length * length,
        ),
    )(qkv, gains, cosine, sine)


class Plan:
    def __init__(self):
        self.operands = []
        self.chunks = []

    def add(self, array):
        self.operands.append(array)
        return len(self.operands) - 1


def fetch(chunk, refs, target, sems, place, along):
    copies = []
    for n, (op, lead, js, jb) in enumerate(chunk):
        source = refs[op]
        for index in lead:
            source = source.at[index]
        head = source.shape[along]
        first = pl.multiple_of(place(js, jb) * head, head)
        spot = (pl.ds(first, head), slice(None)) if along == 0 else (slice(None), pl.ds(first, head))
        copies.append(pltpu.make_async_copy(source, target.at[spot], sems.at[n]))
    return copies


def post_kernel(attn_plan, plan, seqs, n_attn, n_out, scal, noise_ref, *refs):
    attn_refs, refs = refs[:n_attn], refs[n_attn:]
    out_refs, refs = refs[:n_out], refs[n_out:]
    noisy_ref, target_ref, shift_ref, term_ref, grad_ref, part_ref = refs[:6]
    heads, weights, attn_sems, sems = refs[6:]
    i = pl.program_id(0)
    seq, branch = scal[0], scal[1]

    def place(js, jb):
        return (branch ^ jb) * seqs + (seq ^ js)

    def chunk_copies(k):
        return fetch(plan[k], out_refs, weights.at[k % 2], sems.at[k % 2], place, 0)

    @pl.when(i == 0)
    def _():
        copies = fetch(attn_plan, attn_refs, heads, attn_sems, place, 1)
        for copy in copies + chunk_copies(0):
            copy.start()
        for copy in copies:
            copy.wait()
        grad_ref[...] = jnp.zeros_like(grad_ref)

    for k in range(len(plan)):
        @pl.when(i == k)
        def _():
            if k + 1 < len(plan):
                for copy in chunk_copies(k + 1):
                    copy.start()
            for copy in chunk_copies(k):
                copy.wait()

    slot = i % 2
    noise = noise_ref[0]
    head = heads.shape[1] // (plan_heads(plan))
    own = pl.ds(pl.multiple_of(branch * (seqs * head), head), seqs * head)
    term = dot(heads[...], weights[slot])
    term_ref[0] = term
    latent = noisy_ref[...].astype(F32)
    fake_pred = latent - noise * (latent + shift_ref[...] + term)
    cotangent = (-noise * (fake_pred - target_ref[...].astype(F32)) / 64.0).astype(BF16)
    grad_ref[...] += contract(cotangent, weights[slot, own, :], 1, 1)
    part_ref[0] = contract(heads[:, own], cotangent, 0, 0).astype(BF16)


def plan_heads(plan):
    return len(plan[0])


def post(attn, out, scal, noise, noisy, target, shift, seqs, head):
    rows = target.shape[0]
    total = plan_heads(out.chunks)
    cols = out.operands[0].shape[-1]
    count = len(out.chunks)
    n_attn, n_out = len(attn.operands), len(out.operands)
    return pl.pallas_call(
        functools.partial(post_kernel, attn.chunks[0], out.chunks, seqs, n_attn, n_out),
        grid_spec=pltpu.PrefetchScalarGridSpec(
            num_scalar_prefetch=1,
            grid=(count,),
            in_specs=[SMEM]
            + [ANY] * (n_attn + n_out)
            + [
                pl.BlockSpec((rows, cols), lambda i, s: (s[0], s[2 + i])),
                pl.BlockSpec((rows, cols), lambda i, s: (0, s[2 + i])),
                pl.BlockSpec((1, cols), lambda i, s: (0, s[2 + i])),
            ],
            out_specs=[
                pl.BlockSpec((1, rows, cols), lambda i, s: (i, 0, 0)),
                pl.BlockSpec((rows, seqs * head), lambda i, s: (0, 0)),
                pl.BlockSpec((1, seqs * head, cols), lambda i, s: (i, 0, 0)),
            ],
            scratch_shapes=[
                pltpu.VMEM((rows, total * head), BF16),
                pltpu.VMEM((2, total * head, cols), BF16),
                pltpu.SemaphoreType.DMA((total,)),
                pltpu.SemaphoreType.DMA((2, total)),
            ],
        ),
        out_shape=[
            jax.ShapeDtypeStruct((count, rows, cols), F32),
            jax.ShapeDtypeStruct((rows, seqs * head), F32),
            jax.ShapeDtypeStruct((count, seqs * head, cols), BF16),
        ],
        cost_estimate=pl.CostEstimate(
            flops=2 * rows * count * cols * head * (total + 2 * seqs),
            bytes_accessed=count * cols * (2 * total * head + 8 * rows),
            transcendentals=0,
        ),
    )(scal, noise, *attn.operands, *out.operands, noisy, target, shift)


def guide_kernel(attn_plan, plan, seqs, n_attn, n_out, scal, noise_ref, *refs):
    attn_refs, refs = refs[:n_attn], refs[n_attn:]
    out_refs, refs = refs[:n_out], refs[n_out:]
    noisy_ref, target_ref, cond_ref, null_ref, first_ref, second_ref, diff_ref, sum_ref = refs[:8]
    heads, weights, attn_sems, sems = refs[8:]
    i = pl.program_id(0)
    seq, branch = scal[0], scal[1]

    def place(js, jb):
        return (branch ^ jb) * seqs + (seq ^ js)

    def chunk_copies(k):
        return fetch(plan[k], out_refs, weights.at[k % 2], sems.at[k % 2], place, 0)

    @pl.when(i == 0)
    def _():
        copies = fetch(attn_plan, attn_refs, heads, attn_sems, place, 1)
        for copy in copies + chunk_copies(0):
            copy.start()
        for copy in copies:
            copy.wait()
        sum_ref[...] = jnp.zeros_like(sum_ref)

    for k in range(len(plan)):
        @pl.when(i == k)
        def _():
            if k + 1 < len(plan):
                for copy in chunk_copies(k + 1):
                    copy.start()
            for copy in chunk_copies(k):
                copy.wait()

    slot = i % 2
    noise = noise_ref[0]
    guided = dot(heads[...], weights[slot])
    latent = noisy_ref[...].astype(F32)
    cond = latent + cond_ref[...]
    null = latent + null_ref[...]
    real_pred = latent - noise * (guidance * cond - (guidance - 1.0) * null + guided)
    distance = jnp.abs(real_pred - target_ref[...].astype(F32))
    sum_ref[...] += jnp.sum(distance.reshape(-1, 8, distance.shape[1]), axis=0)

    @pl.when(slot == 0)
    def _():
        diff_ref[...] = (latent - noise * (cond + first_ref[0])) - real_pred

    @pl.when(slot == 1)
    def _():
        diff_ref[...] = (latent - noise * (cond + second_ref[0])) - real_pred


def guide(attn, out, scal, noise, noisy, target, cond, null, first, second, seqs, head):
    rows, width = target.shape
    total = plan_heads(out.chunks)
    cols = out.operands[0].shape[-1]
    count = len(out.chunks)
    n_attn, n_out = len(attn.operands), len(out.operands)
    return pl.pallas_call(
        functools.partial(guide_kernel, attn.chunks[0], out.chunks, seqs, n_attn, n_out),
        grid_spec=pltpu.PrefetchScalarGridSpec(
            num_scalar_prefetch=1,
            grid=(count,),
            in_specs=[SMEM]
            + [ANY] * (n_attn + n_out)
            + [
                pl.BlockSpec((rows, cols), lambda i, s: (s[0], s[2 + i])),
                pl.BlockSpec((rows, cols), lambda i, s: (0, s[2 + i])),
                pl.BlockSpec((1, cols), lambda i, s: (0, s[2 + i])),
                pl.BlockSpec((1, cols), lambda i, s: (0, s[2 + i])),
                pl.BlockSpec((1, rows, cols), lambda i, s: (i // 2, 0, 0)),
                pl.BlockSpec((1, rows, cols), lambda i, s: (i // 2, 0, 0)),
            ],
            out_specs=[
                pl.BlockSpec((rows, cols), lambda i, s: (0, s[2 + i])),
                pl.BlockSpec((8, cols), lambda i, s: (0, 0)),
            ],
            scratch_shapes=[
                pltpu.VMEM((rows, total * head), BF16),
                pltpu.VMEM((2, total * head, cols), BF16),
                pltpu.SemaphoreType.DMA((total,)),
                pltpu.SemaphoreType.DMA((2, total)),
            ],
        ),
        out_shape=[jax.ShapeDtypeStruct((rows, width), F32), jax.ShapeDtypeStruct((8, cols), F32)],
        cost_estimate=pl.CostEstimate(
            flops=2 * rows * width * head * total,
            bytes_accessed=width * (2 * total * head + 12 * rows),
            transcendentals=0,
        ),
    )(scal, noise, *attn.operands, *out.operands, noisy, target, cond, null, first, second)


def backward_kernel(
    q_ref, k_ref, v_ref, go_ref, qkv_ref, gain_ref, cos_ref, sin_ref, out_ref, key_sum, value_sum
):
    tile, head = q_ref.shape
    scale = head ** (-0.5)
    i = pl.program_id(0)
    at = pl.ds(pl.multiple_of(i * tile, tile), tile)

    @pl.when(i == 0)
    def _():
        key_sum[...] = jnp.zeros_like(key_sum)
        value_sum[...] = jnp.zeros_like(value_sum)

    def unroll(raw, grad_rot, gain, cosine, sine):
        grad_normed = grad_rot * cosine + rotate_back(grad_rot * sine)
        inverse = lax.rsqrt(jnp.mean(raw * raw, axis=-1, keepdims=True) + norm_eps)
        scaled = gain * grad_normed
        mean = jnp.mean(scaled * raw, axis=-1, keepdims=True)
        return inverse * scaled - raw * inverse * inverse * inverse * mean

    probability = softmax_rows(q_ref[...], k_ref[...], scale)
    grad_prob = contract(go_ref[...], v_ref[...], 1, 1)
    inner = jnp.sum(grad_prob * probability, axis=-1, keepdims=True)
    grad_score = (probability * (grad_prob - inner) * scale).astype(BF16)
    grad_query = unroll(
        qkv_ref[0, at, :head],
        dot(grad_score, k_ref[...]),
        gain_ref[0:1, :],
        cos_ref[at, :],
        sin_ref[at, :],
    )
    out_ref[:head, at] = grad_query.T.astype(BF16)
    key_sum[...] += contract(grad_score, q_ref[...], 0, 0)
    value_sum[...] += contract(probability.astype(BF16), go_ref[...], 0, 0)

    @pl.when(i == pl.num_programs(0) - 1)
    def _():
        grad_key = unroll(
            qkv_ref[0, :, head : 2 * head],
            key_sum[...],
            gain_ref[1:2, :],
            cos_ref[...],
            sin_ref[...],
        )
        out_ref[head : 2 * head, :] = grad_key.T.astype(BF16)
        out_ref[2 * head :, :] = value_sum[...].T.astype(BF16)


def backward(query, key, value, grad_attn, qkv, gains, cosine, sine):
    length, head = query.shape
    tile = min(256, length)
    row = pl.BlockSpec((tile, head), lambda i: (i, 0))
    return pl.pallas_call(
        backward_kernel,
        grid=(length // tile,),
        in_specs=[
            row,
            resident((length, head)),
            resident((length, head)),
            row,
            resident(qkv.shape),
            resident(gains.shape),
            resident(cosine.shape),
            resident(sine.shape),
        ],
        out_specs=pl.BlockSpec((3 * head, length), lambda i: (0, 0)),
        out_shape=jax.ShapeDtypeStruct((3 * head, length), BF16),
        scratch_shapes=[pltpu.VMEM((length, head), F32), pltpu.VMEM((length, head), F32)],
        cost_estimate=pl.CostEstimate(
            flops=20 * length * length * head,
            bytes_accessed=12 * length * head,
            transcendentals=length * length,
        ),
    )(query, key, value, grad_attn, qkv, gains, cosine, sine)


def weight_kernel(scal, grad_ref, hidden_ref, out_ref):
    out_ref[0] = dot(grad_ref[...], hidden_ref[...]).astype(BF16)


def weight_grad(grads, hidden, blocks, cols):
    features, length = grads.shape
    count = blocks.shape[0]
    parts = 2
    tile = cols // parts
    return pl.pallas_call(
        weight_kernel,
        grid_spec=pltpu.PrefetchScalarGridSpec(
            num_scalar_prefetch=1,
            grid=(count, parts),
            in_specs=[
                pl.BlockSpec((features, length), lambda i, p, s: (0, 0)),
                pl.BlockSpec((length, tile), lambda i, p, s: (0, s[i] * parts + p)),
            ],
            out_specs=pl.BlockSpec((1, features, tile), lambda i, p, s: (i, 0, p)),
        ),
        out_shape=jax.ShapeDtypeStruct((count, features, cols), BF16),
        cost_estimate=pl.CostEstimate(
            flops=2 * count * cols * features * length,
            bytes_accessed=2 * count * cols * (length + features),
            transcendentals=0,
        ),
    )(blocks, grads, hidden)


def spread_heads(value, axis, order, which):
    held, orders = [value], list(order)
    for d in range(1, lax.axis_size(axis)):
        held.append(move(value, axis, d))
        orders += [(js ^ d, jb) if which == 0 else (js, jb ^ d) for js, jb in order]
    return held, orders


def gather_out(weight):
    size = lax.axis_size("rep")
    cols = weight.shape[1] // size
    half = cols // 2
    near, far = 1, [bit for bit in bits_of(size) if bit > 1]
    mine = lax.dynamic_slice_in_dim(weight, lax.axis_index("rep") * cols, cols, 1)[None]
    first, second = Plan(), Plan()
    held, base = spread_heads(mine, "branch", [(0, 0)], 1)
    value = jnp.concatenate([v[:, :, :half] for v in held], axis=0)
    others, order = spread_heads(value, "seq", base, 0)
    pieces = [jnp.concatenate(others, axis=0)]
    for bit in far:
        pieces += [move(piece, "rep", bit) for piece in pieces]
    pieces += [move(piece, "rep", near) for piece in pieces]
    for piece in pieces:
        op = first.add(piece)
        first.chunks.append([(op, (n,), js, jb) for n, (js, jb) in enumerate(order)])

    value, order = jnp.concatenate([v[:, :, half:] for v in held], axis=0)[None], base
    for bit in far:
        value = jnp.concatenate([value, move(value, "rep", bit)], axis=0)
    held = [(value, 0)]
    for bit in bits_of(lax.axis_size("seq")):
        held += [(move(v, "seq", bit), js ^ bit) for v, js in held]
    groups = [held, [(move(v, "rep", near), js) for v, js in held]]
    for group in groups:
        ops = [(second.add(v), js) for v, js in group]
        for q in range(value.shape[0]):
            second.chunks.append(
                [(op, (q, n), js, jb) for op, js in ops for n, (_, jb) in enumerate(order)]
            )
    return first, second


def gather_heads(attended, rows):
    seqs = lax.axis_size("seq")
    mine = lax.axis_index("seq")

    def share(d):
        return lax.dynamic_slice_in_dim(attended, (mine ^ d) * rows, rows, 0)

    held = [share(0)] + [move(share(d), "seq", d) for d in range(1, seqs)]
    value, order = jnp.stack(held), [(d, 0) for d in range(seqs)]
    plan, chunk = Plan(), []
    branch_bits = bits_of(lax.axis_size("branch"))
    for bit in branch_bits[:-1]:
        value = jnp.concatenate([value, move(value, "branch", bit)], axis=0)
        order = order + [(js, jb ^ bit) for js, jb in order]
    op = plan.add(value)
    chunk = [(op, (n,), js, jb) for n, (js, jb) in enumerate(order)]
    for bit in branch_bits[-1:]:
        op = plan.add(move(value, "branch", bit))
        chunk += [(op, (n,), js, jb ^ bit) for n, (js, jb) in enumerate(order)]
    plan.chunks.append(chunk)
    return plan


def body(
    noisy,
    generated,
    caption,
    null_caption,
    caption_drop,
    timestep,
    window_start,
    teacher_qkv,
    teacher_out,
    teacher_gain,
    teacher_qk_gain,
    critic_qkv,
    critic_out,
    critic_gain,
    critic_qk_gain,
):
    length, width = noisy.shape[1:]
    head = critic_out.shape[0]
    seqs, reps = lax.axis_size("seq"), lax.axis_size("rep")
    seq, rep, branch = lax.axis_index("seq"), lax.axis_index("rep"), lax.axis_index("branch")
    rows, cols = length // seqs, width // reps
    fraction = (timestep.astype(F32) + 1.0) / 1001.0
    noise = 5.0 * fraction / (1.0 + 4.0 * fraction)
    used_caption = jnp.where(caption_drop[0] == 1, null_caption, caption[0])
    cond_shift = used_caption.astype(F32)[None, :]
    null_shift = null_caption.astype(F32)[None, :]
    both_shift = jnp.concatenate([cond_shift, null_shift], axis=0)
    latent = noisy[0]
    target = generated[0]

    critic_first, critic_second = gather_out(critic_out)
    cosine, sine = rope_tables(window_start[0], length)
    fake_qkv, hidden = project(latent, cond_shift, critic_gain[None], critic_qkv, True, 0, length)
    fake_attn, fake_q, fake_k, fake_v = attend(fake_qkv, critic_qk_gain, cosine, sine, True)
    fake_plan = gather_heads(fake_attn, rows)
    teacher_first, teacher_second = gather_out(teacher_out)
    half = length // 2
    both_qkv = ()
    for start in (0, half):
        both_qkv = project(
            latent, both_shift, teacher_gain[None], teacher_qkv, False, start, half, into=both_qkv
        )
    (both_qkv,) = both_qkv
    (guided_attn,) = attend(both_qkv, teacher_qk_gain, cosine, sine, False)
    guided_plan = gather_heads(guided_attn, rows)

    far = [bit for bit in bits_of(reps) if bit > 1]
    chunks = [0]
    for bit in far:
        chunks += [j ^ bit for j in chunks]
    chunks += [j ^ 1 for j in chunks]
    order = jnp.array(chunks, jnp.int32) ^ rep
    base = jnp.stack([seq, branch]).astype(jnp.int32)
    first_scal = jnp.concatenate([base, order * 2])
    second_scal = jnp.concatenate([base, order * 2 + 1])
    all_scal = jnp.concatenate([base, (order[:, None] * 2 + jnp.arange(2)[None]).reshape(-1)])
    first_term, first_grad, first_part = post(
        fake_plan, critic_first, first_scal, noise, latent, target, cond_shift, seqs, head
    )
    second_term, second_grad, second_part = post(
        fake_plan, critic_second, second_scal, noise, latent, target, cond_shift, seqs, head
    )

    grad_all = (first_grad + second_grad).astype(BF16)

    def grad_block(d):
        return lax.dynamic_slice_in_dim(grad_all, (seq ^ d) * head, head, 1)

    grad_attn = jnp.zeros((length, head), BF16)
    for d in range(seqs):
        piece = move(grad_block(d), "seq", d) if d else grad_block(0)
        grad_attn = lax.dynamic_update_slice(grad_attn, piece, ((seq ^ d) * rows, 0))

    grads = backward(fake_q, fake_k, fake_v, grad_attn, fake_qkv, critic_qk_gain, cosine, sine)
    kept = len(chunks) // 2
    sent = weight_grad(grads, hidden, order[kept:], cols)
    mine = weight_grad(grads, hidden, order[:kept], cols)

    def reduce_rep(mine, sent):
        moved = move(sent, "rep", 1)
        value = mine.astype(F32) + moved.astype(F32)
        for bit in far[::-1]:
            split = value.shape[0] // 2
            moved = move(value[split:].astype(BF16), "rep", bit)
            value = value[:split] + moved.astype(F32)
        return value[0]

    proj_sum = reduce_rep(mine, sent)
    proj_grad = jnp.transpose(proj_sum.reshape(3, head, cols), (0, 2, 1))

    parts = jnp.concatenate([first_part, second_part], axis=2)
    out_sum = reduce_rep(parts[:kept], parts[kept:])
    out_grad = lax.dynamic_slice_in_dim(out_sum, seq * head, head, 0)
    for d in range(1, seqs):
        block = lax.dynamic_slice_in_dim(out_sum, (seq ^ d) * head, head, 0).astype(BF16)
        out_grad += move(block, "seq", d).astype(F32)

    teacher_plan = Plan()
    shift_ops = len(teacher_first.operands)
    teacher_plan.operands = teacher_first.operands + teacher_second.operands
    for one, two in zip(teacher_first.chunks, teacher_second.chunks):
        teacher_plan.chunks.append(one)
        teacher_plan.chunks.append([(op + shift_ops, lead, js, jb) for op, lead, js, jb in two])
    diff, partial = guide(
        guided_plan,
        teacher_plan,
        all_scal,
        noise,
        latent,
        target,
        cond_shift,
        null_shift,
        first_term,
        second_term,
        seqs,
        head,
    )
    total = jnp.broadcast_to(jnp.sum(partial), (8, 128))
    total = total + sum(move(total, "seq", d) for d in range(1, seqs))
    spread = total[0, 0] / (length * width)
    result = (diff / (spread + 1e-05)).astype(BF16)
    return result[None], proj_grad, out_grad


def solution(mesh):
    in_specs = (
        P("rep", None, None),
        P("rep", "seq", None),
        P("rep", None),
        P(),
        P("rep"),
        P("rep"),
        P("rep"),
        P(None, None, ("branch", "seq")),
        P(("branch", "seq"), None),
        P(),
        P(None, ("branch", "seq")),
        P(None, None, ("branch", "seq")),
        P(("branch", "seq"), None),
        P(),
        P(None, ("branch", "seq")),
    )
    out_specs = (
        P("rep", "seq", None),
        P(None, "rep", ("branch", "seq")),
        P(("branch", "seq"), "rep"),
    )
    return jax.shard_map(
        body,
        mesh=mesh,
        in_specs=in_specs,
        out_specs=out_specs,
        check_vma=False,
    )
```

```python
import functools
import jax
import jax.numpy as jnp
from jax import lax
from jax.experimental import pallas as pl
from jax.experimental.pallas import tpu as pltpu
from jax.sharding import PartitionSpec as P

GRID_H = 30
GRID_W = 52

guidance = 5.0
norm_eps = 1e-06

ANY = pl.BlockSpec(memory_space=pl.ANY)
SMEM = pl.BlockSpec(memory_space=pltpu.SMEM)
F32, BF16 = jnp.float32, jnp.bfloat16


def swap(size, bit):
    return [(i, i ^ bit) for i in range(size)]


def bits_of(size):
    return [1 << k for k in range(size.bit_length() - 1)]


def move(value, axis, bit):
    return lax.ppermute(value, axis, swap(lax.axis_size(axis), bit))


def rope_tables(first_token, length):
    token_index = first_token + jnp.arange(length, dtype=jnp.int32)
    plane_size = GRID_H * GRID_W
    frame_index = token_index // plane_size
    remainder = token_index - frame_index * plane_size
    row_index = remainder // GRID_W
    column_index = remainder - row_index * GRID_W
    pair_index = jnp.arange(64, dtype=jnp.int32)
    in_frames = pair_index < 22
    in_rows = jnp.logical_and(pair_index >= 22, pair_index < 43)
    local_rank = jnp.where(
        in_frames, pair_index, jnp.where(in_rows, pair_index - 22, pair_index - 43)
    ).astype(jnp.float32)
    axis_width = jnp.where(in_frames, 44.0, 42.0).astype(jnp.float32)
    frequency = jnp.exp(-jnp.log(10000.0) * 2.0 * local_rank / axis_width)
    chosen = jnp.where(
        in_frames[None, :],
        frame_index[:, None],
        jnp.where(in_rows[None, :], row_index[:, None], column_index[:, None]),
    ).astype(jnp.float32)
    angles = chosen * frequency[None, :]
    angles = jnp.concatenate([angles, angles], axis=1)
    return (jnp.cos(angles), jnp.sin(angles))


def dot(left, right):
    return jnp.dot(left, right, preferred_element_type=F32)


def contract(left, right, left_dim, right_dim):
    return lax.dot_general(
        left, right, (((left_dim,), (right_dim,)), ((), ())), preferred_element_type=F32
    )


def rotate_half(values):
    half = values.shape[-1] // 2
    return jnp.concatenate([-values[..., half:], values[..., :half]], axis=-1)


def rotate_back(values):
    half = values.shape[-1] // 2
    return jnp.concatenate([values[..., half:], -values[..., :half]], axis=-1)


def resident(shape):
    return pl.BlockSpec(shape, lambda *_: (0,) * len(shape), pipeline_mode=pl.Buffered(1))


def project_kernel(variants, keep, noisy_ref, shift_ref, gain_ref, weight_ref, *refs):
    out_ref = refs[0]
    hidden_ref = refs[1] if keep else None
    joined, normed = refs[-2:]
    tile, width = noisy_ref.shape
    head = weight_ref.shape[2]

    @pl.when(pl.program_id(0) == 0)
    def _():
        for k in range(3):
            joined[:, k * head : (k + 1) * head] = weight_ref[k]

    def step(t, carry):
        for u in range(2):
            at = pl.ds(pl.multiple_of(t * 32 + u * 16, 16), 16)
            latent = noisy_ref[at, :].astype(F32)
            for v in range(variants):
                shifted = latent + shift_ref[v : v + 1, :]
                mean = jnp.sum(shifted * shifted, axis=-1, keepdims=True) / width
                scaled = shifted * lax.rsqrt(mean + norm_eps) * gain_ref[...]
                normed[v, at, :] = scaled.astype(BF16)
        return carry

    lax.fori_loop(0, tile // 32, step, 0)
    for v in range(variants):
        out_ref[v] = dot(normed[v], joined[...])
    if keep:
        hidden_ref[...] = normed[0]


def project(noisy, shifts, gain, weight, keep):
    length, width = noisy.shape
    head = weight.shape[2]
    variants = shifts.shape[0]
    tile = min(256, length)
    out_shape = [jax.ShapeDtypeStruct((variants, length, 3 * head), F32)]
    out_specs = [pl.BlockSpec((variants, tile, 3 * head), lambda i: (0, i, 0))]
    if keep:
        out_shape.append(jax.ShapeDtypeStruct((length, width), BF16))
        out_specs.append(pl.BlockSpec((tile, width), lambda i: (i, 0)))
    return pl.pallas_call(
        functools.partial(project_kernel, variants, keep),
        grid=(length // tile,),
        in_specs=[
            pl.BlockSpec((tile, width), lambda i: (i, 0)),
            resident((variants, width)),
            resident((1, width)),
            resident(weight.shape),
        ],
        out_specs=out_specs,
        out_shape=out_shape,
        scratch_shapes=[
            pltpu.VMEM((width, 3 * head), BF16),
            pltpu.VMEM((variants, tile, width), BF16),
        ],
        cost_estimate=pl.CostEstimate(
            flops=2 * variants * length * width * 3 * head,
            bytes_accessed=2 * length * width * (2 if keep else 1) + 6 * width * head,
            transcendentals=0,
        ),
    )(noisy, shifts, gain, weight)


def rope_rows(raw, gain, cosine, sine):
    inverse = lax.rsqrt(jnp.mean(raw * raw, axis=-1, keepdims=True) + norm_eps)
    normed = raw * inverse * gain
    return (normed * cosine + rotate_half(normed) * sine).astype(BF16)


def softmax_rows(query, key, scale):
    exponent = jnp.exp(contract(query, key, 1, 1) * scale)
    return exponent / jnp.sum(exponent, axis=-1, keepdims=True)


def attend_kernel(variants, seqs, per, scal, qkv_ref, gain_ref, cos_ref, sin_ref, *refs):
    shares, saves = refs[:seqs], refs[seqs:-2]
    keys, values = refs[-2:]
    tile, head = shares[0].shape
    scale = head ** (-0.5)
    i = pl.program_id(0)

    @pl.when(i == 0)
    def _():
        for v in range(variants):
            keys[v] = rope_rows(
                qkv_ref[v, :, head : 2 * head], gain_ref[1:2, :], cos_ref[...], sin_ref[...]
            )
            values[v] = qkv_ref[v, :, 2 * head :].astype(BF16)
        if saves:
            saves[1][...] = keys[0]
            saves[2][...] = values[0]

    at = pl.ds(pl.multiple_of(i * tile, tile), tile)
    results = []
    for v in range(variants):
        query = rope_rows(qkv_ref[v, at, :head], gain_ref[0:1, :], cos_ref[at, :], sin_ref[at, :])
        if saves:
            saves[0][...] = query
        prob = softmax_rows(query, keys[v], scale).astype(BF16)
        results.append(dot(prob, values[v]).astype(BF16))
    result = results[0]
    if variants > 1:
        guided = guidance * results[0].astype(F32) - (guidance - 1.0) * results[1].astype(F32)
        result = guided.astype(BF16)
    for d, share in enumerate(shares):

        @pl.when(i // per == (scal[0] ^ d))
        def _():
            share[...] = result


def attend(scal, seqs, qkv, gains, cosine, sine, keep):
    variants, length, triple = qkv.shape
    head = triple // 3
    rows = length // seqs
    tile = min(256, rows)
    per = rows // tile
    saved = 3 if keep else 0
    row = pl.BlockSpec((tile, head), lambda i, s: (i, 0))
    whole = pl.BlockSpec((length, head), lambda i, s: (0, 0))
    flat = jax.ShapeDtypeStruct((length, head), BF16)

    def share(d):
        return pl.BlockSpec(
            (tile, head), lambda i, s: (jnp.clip(i - (s[0] ^ d) * per, 0, per - 1), 0)
        )

    results = pl.pallas_call(
        functools.partial(attend_kernel, variants, seqs, per),
        grid_spec=pltpu.PrefetchScalarGridSpec(
            num_scalar_prefetch=1,
            grid=(length // tile,),
            in_specs=[
                resident(qkv.shape),
                resident(gains.shape),
                resident(cosine.shape),
                resident(sine.shape),
            ],
            out_specs=[share(d) for d in range(seqs)] + [row, whole, whole][:saved],
            scratch_shapes=[
                pltpu.VMEM((variants, length, head), BF16),
                pltpu.VMEM((variants, length, head), BF16),
            ],
        ),
        out_shape=[jax.ShapeDtypeStruct((rows, head), BF16)] * seqs + [flat] * saved,
        cost_estimate=pl.CostEstimate(
            flops=16 * variants * length * length * head,
            bytes_accessed=4 * variants * length * triple,
            transcendentals=variants * length * length,
        ),
    )(scal, qkv, gains, cosine, sine)
    return results[:seqs], results[seqs:]


class Plan:
    def __init__(self):
        self.operands = []
        self.chunks = []

    def add(self, array):
        self.operands.append(array)
        return len(self.operands) - 1


def fetch(chunk, refs, target, sems, place, along, columns=None):
    copies = []
    for n, (op, lead, js, jb) in enumerate(chunk):
        source = refs[op]
        for index in lead:
            source = source.at[index]
        if columns is not None:
            source = source.at[:, columns]
        head = source.shape[along]
        first = pl.multiple_of(place(js, jb) * head, head)
        spot = (pl.ds(first, head), slice(None)) if along == 0 else (slice(None), pl.ds(first, head))
        copies.append(pltpu.make_async_copy(source, target.at[spot], sems.at[n]))
    return copies


def stream(attn_plan, plan, seqs, scal, attn_refs, out_refs, heads, weights, attn_sems, sems):
    i = pl.program_id(0)
    seq, branch = scal[0], scal[1]
    cols = weights.shape[2]

    def place(js, jb):
        return (branch ^ jb) * seqs + (seq ^ js)

    def copies_of(k):
        columns = pl.ds((k % 2) * cols, cols)
        return fetch(plan[k // 2], out_refs, weights.at[k % 2], sems.at[k % 2], place, 0, columns)

    @pl.when(i == 0)
    def _():
        copies = fetch(attn_plan, attn_refs, heads, attn_sems, place, 1)
        for copy in copies + copies_of(0):
            copy.start()
        for copy in copies:
            copy.wait()

    steps = 2 * len(plan)
    for k in range(steps):

        @pl.when(i == k)
        def _():
            if k + 1 < steps:
                for copy in copies_of(k + 1):
                    copy.start()
            for copy in copies_of(k):
                copy.wait()

    return i % 2


def row_blocks(rows):
    block = min(128, rows)
    return [slice(start, start + block) for start in range(0, rows, block)]


def post_kernel(attn_plan, plan, seqs, n_attn, n_out, resume, scal, noise_ref, *refs):
    attn_refs, refs = refs[:n_attn], refs[n_attn:]
    out_refs, refs = refs[:n_out], refs[n_out:]
    noisy_ref, target_ref, shift_ref = refs[:3]
    refs = refs[3:]
    if resume:
        before_ref, refs = refs[0], refs[1:]
    term_ref, part_ref, grad_ref = refs[:3]
    heads, weights, cotangents, attn_sems, sems = refs[3:]
    slot = stream(
        attn_plan, plan, seqs, scal, attn_refs, out_refs, heads, weights, attn_sems, sems
    )

    @pl.when(pl.program_id(0) == 0)
    def _():
        grad_ref[...] = before_ref[...] if resume else jnp.zeros_like(grad_ref)

    noise = noise_ref[0]
    own_size = part_ref.shape[1]
    own = pl.ds(pl.multiple_of(scal[1] * own_size, own_size), own_size)
    for at in row_blocks(noisy_ref.shape[0]):
        term = dot(heads[at, :], weights[slot])
        term_ref[0, at, :] = term.astype(BF16)
        latent = noisy_ref[at, :].astype(F32)
        fake_pred = latent - noise * (latent + shift_ref[...] + term)
        cotangent = (noise * (-1.0 / 64.0)) * (fake_pred - target_ref[at, :].astype(F32))
        cotangents[at, :] = cotangent.astype(BF16)
        grad_ref[at, :] += contract(cotangents[at, :], weights[slot, own, :], 1, 1)
    part_ref[0] = contract(heads[:, own], cotangents[...], 0, 0).astype(BF16)


def plan_heads(plan):
    return len(plan[0])


def post(attn, out, blocks, scal, noise, noisy, target, shift, seqs, head, before):
    rows = target.shape[0]
    total = plan_heads(out.chunks)
    cols = out.operands[0].shape[-1] // 2
    chunks = len(out.chunks)
    n_attn, n_out = len(attn.operands), len(out.operands)
    kernel = functools.partial(
        post_kernel, attn.chunks[0], out.chunks, seqs, n_attn, n_out, len(before)
    )
    grad_spec = pl.BlockSpec((rows, seqs * head), lambda i, s: (0, 0))

    def spot(i, s):
        return s[2 + blocks + i // 2] * 2 + i % 2

    return pl.pallas_call(
        kernel,
        grid_spec=pltpu.PrefetchScalarGridSpec(
            num_scalar_prefetch=1,
            grid=(2 * chunks,),
            in_specs=[SMEM]
            + [ANY] * (n_attn + n_out)
            + [
                pl.BlockSpec((rows, cols), lambda i, s: (s[0], spot(i, s))),
                pl.BlockSpec((rows, cols), lambda i, s: (0, spot(i, s))),
                pl.BlockSpec((1, cols), lambda i, s: (0, spot(i, s))),
            ]
            + [grad_spec] * len(before),
            out_specs=[
                pl.BlockSpec((1, rows, cols), lambda i, s: (i // 2, 0, i % 2)),
                pl.BlockSpec((1, seqs * head, cols), lambda i, s: (i // 2, 0, i % 2)),
                grad_spec,
            ],
            scratch_shapes=[
                pltpu.VMEM((rows, total * head), BF16),
                pltpu.VMEM((2, total * head, cols), BF16),
                pltpu.VMEM((rows, cols), BF16),
                pltpu.SemaphoreType.DMA((total,)),
                pltpu.SemaphoreType.DMA((2, total)),
            ],
        ),
        out_shape=[
            jax.ShapeDtypeStruct((chunks, rows, 2 * cols), BF16),
            jax.ShapeDtypeStruct((chunks, seqs * head, 2 * cols), BF16),
            jax.ShapeDtypeStruct((rows, seqs * head), F32),
        ],
        cost_estimate=pl.CostEstimate(
            flops=4 * rows * chunks * cols * head * (total + 2 * seqs),
            bytes_accessed=2 * chunks * cols * (2 * total * head + 8 * rows),
            transcendentals=0,
        ),
    )(scal, noise, *attn.operands, *out.operands, noisy, target, shift, *before)


def guide_kernel(attn_plan, plan, seqs, n_attn, n_out, scal, noise_ref, *refs):
    attn_refs, refs = refs[:n_attn], refs[n_attn:]
    out_refs, refs = refs[:n_out], refs[n_out:]
    noisy_ref, target_ref, cond_ref, null_ref, near_ref, far_ref, diff_ref, total_ref = refs[:8]
    sum_ref, heads, weights, attn_sems, sems = refs[8:]
    slot = stream(
        attn_plan, plan, seqs, scal, attn_refs, out_refs, heads, weights, attn_sems, sems
    )

    @pl.when(pl.program_id(0) == 0)
    def _():
        sum_ref[...] = jnp.zeros_like(sum_ref)

    noise = noise_ref[0]
    own = pl.program_id(0) < pl.num_programs(0) // 2
    cond = cond_ref[...]
    mixed = guidance * cond - (guidance - 1.0) * null_ref[...]
    for at in row_blocks(noisy_ref.shape[0]):
        guided = dot(heads[at, :], weights[slot]) + mixed
        latent = noisy_ref[at, :].astype(F32)
        real_pred = latent - noise * (latent + guided)
        distance = jnp.abs(real_pred - target_ref[at, :].astype(F32))
        sum_ref[...] += jnp.sum(distance.reshape(-1, 8, distance.shape[1]), axis=0)
        term = jnp.where(own, near_ref[0, at, :].astype(F32), far_ref[0, at, :].astype(F32))
        diff_ref[at, :] = (noise * (guided - (cond + term))).astype(BF16)

    @pl.when(pl.program_id(0) == pl.num_programs(0) - 1)
    def _():
        total_ref[...] = jnp.broadcast_to(jnp.sum(sum_ref[...]), total_ref.shape)


def guide(attn, out, scal, noise, noisy, target, cond, null, near, far, seqs, head):
    rows, width = target.shape
    total = plan_heads(out.chunks)
    cols = out.operands[0].shape[-1] // 2
    chunks = len(out.chunks)
    n_attn, n_out = len(attn.operands), len(out.operands)

    def spot(i, s):
        return s[2 + i // 2] * 2 + i % 2

    column = pl.BlockSpec((1, cols), lambda i, s: (0, spot(i, s)))
    last = chunks - 1

    def near_spot(i, s):
        return (jnp.minimum(i, last) // 2, 0, jnp.minimum(i, last) % 2)

    def far_spot(i, s):
        return (jnp.maximum(i - last - 1, 0) // 2, 0, jnp.maximum(i - last - 1, 0) % 2)

    return pl.pallas_call(
        functools.partial(guide_kernel, attn.chunks[0], out.chunks, seqs, n_attn, n_out),
        grid_spec=pltpu.PrefetchScalarGridSpec(
            num_scalar_prefetch=1,
            grid=(2 * chunks,),
            in_specs=[SMEM]
            + [ANY] * (n_attn + n_out)
            + [
                pl.BlockSpec((rows, cols), lambda i, s: (s[0], spot(i, s))),
                pl.BlockSpec((rows, cols), lambda i, s: (0, spot(i, s))),
                column,
                column,
                pl.BlockSpec((1, rows, cols), near_spot),
                pl.BlockSpec((1, rows, cols), far_spot),
            ],
            out_specs=[
                pl.BlockSpec((rows, cols), lambda i, s: (0, spot(i, s))),
                pl.BlockSpec((8, 128), lambda i, s: (0, 0)),
            ],
            scratch_shapes=[
                pltpu.VMEM((8, cols), F32),
                pltpu.VMEM((rows, total * head), BF16),
                pltpu.VMEM((2, total * head, cols), BF16),
                pltpu.SemaphoreType.DMA((total,)),
                pltpu.SemaphoreType.DMA((2, total)),
            ],
        ),
        out_shape=[jax.ShapeDtypeStruct((rows, width), BF16), jax.ShapeDtypeStruct((8, 128), F32)],
        cost_estimate=pl.CostEstimate(
            flops=2 * rows * width * head * total,
            bytes_accessed=width * (2 * total * head + 8 * rows),
            transcendentals=0,
        ),
    )(scal, noise, *attn.operands, *out.operands, noisy, target, cond, null, near, far)


def backward_kernel(
    q_ref, k_ref, v_ref, go_ref, qkv_ref, gain_ref, cos_ref, sin_ref, out_ref, key_sum, value_sum
):
    tile, head = q_ref.shape
    scale = head ** (-0.5)
    i = pl.program_id(0)
    at = pl.ds(pl.multiple_of(i * tile, tile), tile)

    @pl.when(i == 0)
    def _():
        key_sum[...] = jnp.zeros_like(key_sum)
        value_sum[...] = jnp.zeros_like(value_sum)

    def unroll(raw, grad_rot, gain, cosine, sine):
        grad_normed = grad_rot * cosine + rotate_back(grad_rot * sine)
        inverse = lax.rsqrt(jnp.mean(raw * raw, axis=-1, keepdims=True) + norm_eps)
        scaled = gain * grad_normed
        mean = jnp.mean(scaled * raw, axis=-1, keepdims=True)
        return inverse * scaled - raw * inverse * inverse * inverse * mean

    probability = softmax_rows(q_ref[...], k_ref[...], scale)
    grad_prob = contract(go_ref[...], v_ref[...], 1, 1)
    inner = jnp.sum(grad_prob * probability, axis=-1, keepdims=True)
    grad_score = (probability * (grad_prob - inner) * scale).astype(BF16)
    grad_query = unroll(
        qkv_ref[0, at, :head],
        dot(grad_score, k_ref[...]),
        gain_ref[0:1, :],
        cos_ref[at, :],
        sin_ref[at, :],
    )
    out_ref[:head, at] = grad_query.T.astype(BF16)
    key_sum[...] += contract(grad_score, q_ref[...], 0, 0)
    value_sum[...] += contract(probability.astype(BF16), go_ref[...], 0, 0)

    @pl.when(i == pl.num_programs(0) - 1)
    def _():
        grad_key = unroll(
            qkv_ref[0, :, head : 2 * head],
            key_sum[...],
            gain_ref[1:2, :],
            cos_ref[...],
            sin_ref[...],
        )
        out_ref[head : 2 * head, :] = grad_key.T.astype(BF16)
        out_ref[2 * head :, :] = value_sum[...].T.astype(BF16)


def backward(query, key, value, grad_attn, qkv, gains, cosine, sine):
    length, head = query.shape
    tile = min(256, length)
    row = pl.BlockSpec((tile, head), lambda i: (i, 0))
    return pl.pallas_call(
        backward_kernel,
        grid=(length // tile,),
        in_specs=[
            row,
            resident((length, head)),
            resident((length, head)),
            row,
            resident(qkv.shape),
            resident(gains.shape),
            resident(cosine.shape),
            resident(sine.shape),
        ],
        out_specs=pl.BlockSpec((3 * head, length), lambda i: (0, 0)),
        out_shape=jax.ShapeDtypeStruct((3 * head, length), BF16),
        scratch_shapes=[pltpu.VMEM((length, head), F32), pltpu.VMEM((length, head), F32)],
        cost_estimate=pl.CostEstimate(
            flops=20 * length * length * head,
            bytes_accessed=12 * length * head,
            transcendentals=length * length,
        ),
    )(query, key, value, grad_attn, qkv, gains, cosine, sine)


def weight_kernel(scal, grad_ref, hidden_ref, out_ref):
    out_ref[0] = dot(grad_ref[...], hidden_ref[...]).astype(BF16)


def weight_grad(grads, hidden, blocks, count, scal, cols):
    features, length = grads.shape
    parts = 2
    tile = cols // parts
    return pl.pallas_call(
        weight_kernel,
        grid_spec=pltpu.PrefetchScalarGridSpec(
            num_scalar_prefetch=1,
            grid=(count, parts),
            in_specs=[
                pl.BlockSpec((features, length), lambda i, p, s: (0, 0)),
                pl.BlockSpec((length, tile), lambda i, p, s: (0, s[2 + blocks + i] * parts + p)),
            ],
            out_specs=pl.BlockSpec((1, features, tile), lambda i, p, s: (i, 0, p)),
        ),
        out_shape=jax.ShapeDtypeStruct((count, features, cols), BF16),
        cost_estimate=pl.CostEstimate(
            flops=2 * count * cols * features * length,
            bytes_accessed=2 * count * cols * (length + features),
            transcendentals=0,
        ),
    )(scal, grads, hidden)


def spread_heads(value, axis, order, which):
    held, orders = [value], list(order)
    for d in range(1, lax.axis_size(axis)):
        held.append(move(value, axis, d))
        orders += [(js ^ d, jb) if which == 0 else (js, jb ^ d) for js, jb in order]
    return held, orders


def scale_kernel(entries, *refs):
    diff_ref, out_ref = refs[-2:]
    total = sum(ref[0:1, 0:1] for ref in refs[:-2])
    inverse = 1.0 / (total / entries + 1e-05)
    out_ref[...] = (diff_ref[...].astype(F32) * inverse).astype(BF16)


def scale(diff, totals, entries):
    rows, width = diff.shape
    tile = min(64, rows)
    block = pl.BlockSpec((tile, width), lambda i: (i, 0))
    return pl.pallas_call(
        functools.partial(scale_kernel, entries),
        grid=(rows // tile,),
        in_specs=[resident(totals[0].shape)] * len(totals) + [block],
        out_specs=block,
        out_shape=jax.ShapeDtypeStruct((rows, width), BF16),
        cost_estimate=pl.CostEstimate(
            flops=4 * rows * width, bytes_accessed=4 * rows * width, transcendentals=0
        ),
    )(*totals, diff)


def turn_kernel(*refs):
    terms, out_ref = refs[:-1], refs[-1]
    head = out_ref.shape[2]
    for k in range(3):
        at = slice(k * head, (k + 1) * head)
        value = sum(term[0, at, :].astype(F32) for term in terms)
        out_ref[k] = value.T


def turn(terms, head):
    features, cols = terms[0].shape[1:]
    tile = cols // 2
    return pl.pallas_call(
        turn_kernel,
        grid=(cols // tile,),
        in_specs=[pl.BlockSpec((1, features, tile), lambda i: (0, 0, i))] * len(terms),
        out_specs=pl.BlockSpec((3, tile, head), lambda i: (0, i, 0)),
        out_shape=jax.ShapeDtypeStruct((3, cols, head), F32),
        cost_estimate=pl.CostEstimate(
            flops=3 * features * cols, bytes_accessed=10 * features * cols, transcendentals=0
        ),
    )(*terms)


def gather_out(weight, rep):
    size = lax.axis_size("rep")
    cols = weight.shape[1] // size
    far = [bit for bit in bits_of(size) if bit > 1]
    mine = lax.dynamic_slice_in_dim(weight, rep * cols, cols, 1)[None]
    held, order = spread_heads(mine, "branch", [(0, 0)], 1)
    middle = max(len(held) // 2, 1)
    near_plan, far_plan = Plan(), Plan()
    near_plan.chunks = [[] for _ in range(size // 2)]
    far_plan.chunks = [[] for _ in range(size // 2)]

    def add(value, heads):
        for plan, v in ((near_plan, value), (far_plan, move(value, "rep", 1))):
            op = plan.add(v)
            for chunk, lead, js, jb in heads:
                plan.chunks[chunk].append((op, lead, js, jb))

    value = jnp.concatenate(held[:middle], axis=0)
    others, heads = spread_heads(value, "seq", order[:middle], 0)
    pieces = [jnp.concatenate(others, axis=0)]
    for bit in far:
        pieces += [move(piece, "rep", bit) for piece in pieces]
    for q, piece in enumerate(pieces):
        add(piece, [(q, (n,), js, jb) for n, (js, jb) in enumerate(heads)])

    value = jnp.concatenate(held[middle:], axis=0)[None]
    for bit in far:
        value = jnp.concatenate([value, move(value, "rep", bit)], axis=0)
    seqs = lax.axis_size("seq")
    for d in range(seqs):
        piece = move(value, "seq", d) if d else value
        heads = [
            (q, (q, n), d, jb)
            for q in range(value.shape[0])
            for n, (_, jb) in enumerate(order[middle:])
        ]
        add(piece, heads)
    return near_plan, far_plan


def gather_heads(attended):
    seqs = len(attended)
    held = [attended[0]] + [move(attended[d], "seq", d) for d in range(1, seqs)]
    held, order = spread_heads(jnp.stack(held), "branch", [(d, 0) for d in range(seqs)], 1)
    plan = Plan()
    chunk = []
    for n, (js, jb) in enumerate(order):
        if n % seqs == 0:
            op = plan.add(held[n // seqs])
        chunk.append((op, (n % seqs,), js, jb))
    plan.chunks.append(chunk)
    return plan


def body(
    noisy,
    generated,
    caption,
    null_caption,
    caption_drop,
    timestep,
    window_start,
    teacher_qkv,
    teacher_out,
    teacher_gain,
    teacher_qk_gain,
    critic_qkv,
    critic_out,
    critic_gain,
    critic_qk_gain,
):
    length, width = noisy.shape[1:]
    head = critic_out.shape[0]
    seqs, reps = lax.axis_size("seq"), lax.axis_size("rep")
    seq, rep, branch = lax.axis_index("seq"), lax.axis_index("rep"), lax.axis_index("branch")
    rows, cols = length // seqs, width // reps
    fraction = (timestep.astype(F32) + 1.0) / 1001.0
    noise = 5.0 * fraction / (1.0 + 4.0 * fraction)
    used_caption = jnp.where(caption_drop[0] == 1, null_caption, caption[0])
    cond_shift = used_caption.astype(F32)[None, :]
    null_shift = null_caption.astype(F32)[None, :]
    both_shift = jnp.concatenate([cond_shift, null_shift], axis=0)
    latent = noisy[0]
    target = generated[0]
    far = [bit for bit in bits_of(reps) if bit > 1]
    chunks = [0]
    for bit in far:
        chunks += [j ^ bit for j in chunks]
    kept = len(chunks)
    chunks += [j ^ 1 for j in chunks]
    scal = jnp.stack([seq, branch] + [rep ^ j for j in chunks]).astype(jnp.int32)

    critic_near, critic_far = gather_out(critic_out, rep)
    cosine, sine = rope_tables(window_start[0], length)
    fake_qkv, hidden = project(latent, cond_shift, critic_gain[None], critic_qkv, True)
    later, fake_qkv = lax.optimization_barrier((rep, fake_qkv))
    fake_attn, (fake_q, fake_k, fake_v) = attend(
        scal, seqs, fake_qkv, critic_qk_gain, cosine, sine, True
    )
    fake_plan = gather_heads(fake_attn)
    teacher_near, teacher_far = gather_out(teacher_out, later)
    (both_qkv,) = project(latent, both_shift, teacher_gain[None], teacher_qkv, False)
    guided_attn, _ = attend(scal, seqs, both_qkv, teacher_qk_gain, cosine, sine, False)
    guided_plan = gather_heads(guided_attn)

    common = (noise, latent, target, cond_shift, seqs, head)
    near_term, near_part, near_grad = post(fake_plan, critic_near, 0, scal, *common, ())
    far_term, far_part, grad_all = post(fake_plan, critic_far, kept, scal, *common, (near_grad,))

    def grad_block(d):
        return lax.dynamic_slice_in_dim(grad_all, (seq ^ d) * head, head, 1).astype(BF16)

    grad_attn = jnp.zeros((length, head), BF16)
    for d in range(seqs):
        piece = move(grad_block(d), "seq", d) if d else grad_block(0)
        grad_attn = lax.dynamic_update_slice(grad_attn, piece, ((seq ^ d) * rows, 0))

    grads = backward(fake_q, fake_k, fake_v, grad_attn, fake_qkv, critic_qk_gain, cosine, sine)
    far_weight = weight_grad(grads, hidden, kept, kept, scal, cols)
    near_weight = weight_grad(grads, hidden, 0, kept, scal, cols)

    def reduce_rep(kept_part, sent_part):
        terms = [kept_part, move(sent_part, "rep", 1)]
        for bit in far[::-1]:
            split = bit // 2
            upper = sum(term[split : 2 * split].astype(F32) for term in terms).astype(BF16)
            terms = terms + [move(upper, "rep", bit)]
        return terms

    terms = reduce_rep(near_part, far_part)

    def out_block(d):
        return sum(
            lax.dynamic_slice(term, (0, (seq ^ d) * head, 0), (1, head, cols))[0].astype(F32)
            for term in terms
        )

    out_grad = out_block(0)
    for d in range(1, seqs):
        out_grad += move(out_block(d).astype(BF16), "seq", d).astype(F32)

    proj_terms = reduce_rep(near_weight, far_weight)
    proj_grad = turn(proj_terms, head)

    teacher_plan = Plan()
    shift_ops = len(teacher_near.operands)
    teacher_plan.operands = teacher_near.operands + teacher_far.operands
    teacher_plan.chunks = teacher_near.chunks + [
        [(op + shift_ops, lead, js, jb) for op, lead, js, jb in chunk]
        for chunk in teacher_far.chunks
    ]
    diff, partial = guide(
        guided_plan,
        teacher_plan,
        scal,
        noise,
        latent,
        target,
        cond_shift,
        null_shift,
        near_term,
        far_term,
        seqs,
        head,
    )
    totals = [partial] + [move(partial, "seq", d) for d in range(1, seqs)]
    result = scale(diff, totals, length * width)
    return result[None], proj_grad, out_grad


def solution(mesh):
    in_specs = (
        P("rep", None, None),
        P("rep", "seq", None),
        P("rep", None),
        P(),
        P("rep"),
        P("rep"),
        P("rep"),
        P(None, None, ("branch", "seq")),
        P(("branch", "seq"), None),
        P(),
        P(None, ("branch", "seq")),
        P(None, None, ("branch", "seq")),
        P(("branch", "seq"), None),
        P(),
        P(None, ("branch", "seq")),
    )
    out_specs = (
        P("rep", "seq", None),
        P(None, "rep", ("branch", "seq")),
        P(("branch", "seq"), "rep"),
    )
    return jax.shard_map(
        body,
        mesh=mesh,
        in_specs=in_specs,
        out_specs=out_specs,
        check_vma=False,
    )
```

```python
import functools
import jax
import jax.numpy as jnp
from jax import lax
from jax.experimental import pallas as pl
from jax.experimental.pallas import tpu as pltpu
from jax.sharding import PartitionSpec as P

GRID_H = 30
GRID_W = 52

guidance = 5.0
norm_eps = 1e-06

ANY = pl.BlockSpec(memory_space=pl.ANY)
SMEM = pl.BlockSpec(memory_space=pltpu.SMEM)
F32, BF16 = jnp.float32, jnp.bfloat16
GRANT = pltpu.CompilerParams(vmem_limit_bytes=32 << 20)


def swap(size, bit):
    return [(i, i ^ bit) for i in range(size)]


def bits_of(size):
    return [1 << k for k in range(size.bit_length() - 1)]


def move(value, axis, bit):
    return lax.ppermute(value, axis, swap(lax.axis_size(axis), bit))


def rope_tables(first_token, length):
    token_index = first_token + jnp.arange(length, dtype=jnp.int32)
    plane_size = GRID_H * GRID_W
    frame_index = token_index // plane_size
    remainder = token_index - frame_index * plane_size
    row_index = remainder // GRID_W
    column_index = remainder - row_index * GRID_W
    pair_index = jnp.arange(64, dtype=jnp.int32)
    in_frames = pair_index < 22
    in_rows = jnp.logical_and(pair_index >= 22, pair_index < 43)
    local_rank = jnp.where(
        in_frames, pair_index, jnp.where(in_rows, pair_index - 22, pair_index - 43)
    ).astype(jnp.float32)
    axis_width = jnp.where(in_frames, 44.0, 42.0).astype(jnp.float32)
    frequency = jnp.exp(-jnp.log(10000.0) * 2.0 * local_rank / axis_width)
    chosen = jnp.where(
        in_frames[None, :],
        frame_index[:, None],
        jnp.where(in_rows[None, :], row_index[:, None], column_index[:, None]),
    ).astype(jnp.float32)
    angles = chosen * frequency[None, :]
    angles = jnp.concatenate([angles, angles], axis=1)
    return (jnp.cos(angles), jnp.sin(angles))


def dot(left, right):
    return jnp.dot(left, right, preferred_element_type=F32)


def contract(left, right, left_dim, right_dim):
    return lax.dot_general(
        left, right, (((left_dim,), (right_dim,)), ((), ())), preferred_element_type=F32
    )


def rotate_half(values):
    half = values.shape[-1] // 2
    return jnp.concatenate([-values[..., half:], values[..., :half]], axis=-1)


def rotate_back(values):
    half = values.shape[-1] // 2
    return jnp.concatenate([values[..., half:], -values[..., :half]], axis=-1)


def resident(shape):
    return pl.BlockSpec(shape, lambda *_: (0,) * len(shape), pipeline_mode=pl.Buffered(1))


def project_kernel(variants, keep, held, noisy_ref, shift_ref, gain_ref, weight_ref, *refs):
    refs = refs[held:]
    out_ref = refs[0]
    hidden_ref = refs[1] if keep else None
    joined, normed = refs[-2:]
    tile, width = noisy_ref.shape
    head = weight_ref.shape[2]

    @pl.when(pl.program_id(0) == 0)
    def _():
        for k in range(3):
            joined[:, k * head : (k + 1) * head] = weight_ref[k]

    def step(t, carry):
        for u in range(2):
            at = pl.ds(pl.multiple_of(t * 32 + u * 16, 16), 16)
            latent = noisy_ref[at, :].astype(F32)
            for v in range(variants):
                shifted = latent + shift_ref[v : v + 1, :]
                mean = jnp.sum(shifted * shifted, axis=-1, keepdims=True) / width
                scaled = shifted * lax.rsqrt(mean + norm_eps) * gain_ref[...]
                normed[v, at, :] = scaled.astype(BF16)
        return carry

    lax.fori_loop(0, tile // 32, step, 0)
    for v in range(variants):
        out_ref[v] = dot(normed[v], joined[...])
    if keep:
        hidden_ref[...] = normed[0]


def project(noisy, shifts, gain, weight, keep, start, count, into=()):
    length, width = noisy.shape
    head = weight.shape[2]
    variants = shifts.shape[0]
    tile = min(256, count)
    first = start // tile
    out_shape = [jax.ShapeDtypeStruct((variants, length, 3 * head), F32)]
    out_specs = [pl.BlockSpec((variants, tile, 3 * head), lambda i: (0, first + i, 0))]
    if keep:
        out_shape.append(jax.ShapeDtypeStruct((length, width), BF16))
        out_specs.append(pl.BlockSpec((tile, width), lambda i: (first + i, 0)))
    return pl.pallas_call(
        functools.partial(project_kernel, variants, keep, len(into)),
        grid=(count // tile,),
        in_specs=[
            pl.BlockSpec((tile, width), lambda i: (first + i, 0)),
            resident((variants, width)),
            resident((1, width)),
            resident(weight.shape),
        ]
        + [ANY] * len(into),
        out_specs=out_specs,
        out_shape=out_shape,
        input_output_aliases={4 + n: n for n in range(len(into))},
        scratch_shapes=[
            pltpu.VMEM((width, 3 * head), BF16),
            pltpu.VMEM((variants, tile, width), BF16),
        ],
        cost_estimate=pl.CostEstimate(
            flops=2 * variants * count * width * 3 * head,
            bytes_accessed=2 * count * width * (2 if keep else 1) + 6 * width * head,
            transcendentals=0,
        ),
    )(noisy, shifts, gain, weight, *into)


def rope_rows(raw, gain, cosine, sine):
    inverse = lax.rsqrt(jnp.mean(raw * raw, axis=-1, keepdims=True) + norm_eps)
    normed = raw * inverse * gain
    return (normed * cosine + rotate_half(normed) * sine).astype(BF16)


def softmax_rows(query, key, scale):
    exponent = jnp.exp(contract(query, key, 1, 1) * scale)
    return exponent / jnp.sum(exponent, axis=-1, keepdims=True)


def attend_kernel(variants, seqs, per, scal, qkv_ref, gain_ref, cos_ref, sin_ref, *refs):
    shares, saves = refs[:seqs], refs[seqs:-2]
    keys, values = refs[-2:]
    tile, head = shares[0].shape
    scale = head ** (-0.5)
    i = pl.program_id(0)

    @pl.when(i == 0)
    def _():
        for v in range(variants):
            keys[v] = rope_rows(
                qkv_ref[v, :, head : 2 * head], gain_ref[1:2, :], cos_ref[...], sin_ref[...]
            )
            values[v] = qkv_ref[v, :, 2 * head :].astype(BF16)
        if saves:
            saves[1][...] = keys[0]
            saves[2][...] = values[0]

    at = pl.ds(pl.multiple_of(i * tile, tile), tile)
    results = []
    for v in range(variants):
        query = rope_rows(qkv_ref[v, at, :head], gain_ref[0:1, :], cos_ref[at, :], sin_ref[at, :])
        if saves:
            saves[0][...] = query
        prob = softmax_rows(query, keys[v], scale).astype(BF16)
        results.append(dot(prob, values[v]).astype(BF16))
    result = results[0]
    if variants > 1:
        guided = guidance * results[0].astype(F32) - (guidance - 1.0) * results[1].astype(F32)
        result = guided.astype(BF16)
    for d, share in enumerate(shares):

        @pl.when(i // per == (scal[0] ^ d))
        def _():
            share[...] = result


def attend(scal, seqs, qkv, gains, cosine, sine, keep):
    variants, length, triple = qkv.shape
    head = triple // 3
    rows = length // seqs
    tile = min(256, rows)
    per = rows // tile
    saved = 3 if keep else 0
    row = pl.BlockSpec((tile, head), lambda i, s: (i, 0))
    whole = pl.BlockSpec((length, head), lambda i, s: (0, 0))
    flat = jax.ShapeDtypeStruct((length, head), BF16)

    def share(d):
        return pl.BlockSpec(
            (tile, head), lambda i, s: (jnp.clip(i - (s[0] ^ d) * per, 0, per - 1), 0)
        )

    results = pl.pallas_call(
        functools.partial(attend_kernel, variants, seqs, per),
        grid_spec=pltpu.PrefetchScalarGridSpec(
            num_scalar_prefetch=1,
            grid=(length // tile,),
            in_specs=[
                resident(qkv.shape),
                resident(gains.shape),
                resident(cosine.shape),
                resident(sine.shape),
            ],
            out_specs=[share(d) for d in range(seqs)] + [row, whole, whole][:saved],
            scratch_shapes=[
                pltpu.VMEM((variants, length, head), BF16),
                pltpu.VMEM((variants, length, head), BF16),
            ],
        ),
        out_shape=[jax.ShapeDtypeStruct((rows, head), BF16)] * seqs + [flat] * saved,
        cost_estimate=pl.CostEstimate(
            flops=16 * variants * length * length * head,
            bytes_accessed=4 * variants * length * triple,
            transcendentals=variants * length * length,
        ),
    )(scal, qkv, gains, cosine, sine)
    return results[:seqs], results[seqs:]


class Plan:
    def __init__(self):
        self.operands = []
        self.chunks = []

    def add(self, array):
        self.operands.append(array)
        return len(self.operands) - 1


def fetch(chunk, refs, target, sems, place, along, columns=None):
    copies = []
    for n, (op, lead, js, jb) in enumerate(chunk):
        source = refs[op]
        for index in lead:
            source = source.at[index]
        if columns is not None:
            source = source.at[:, columns]
        head = source.shape[along]
        first = pl.multiple_of(place(js, jb) * head, head)
        spot = (pl.ds(first, head), slice(None)) if along == 0 else (slice(None), pl.ds(first, head))
        copies.append(pltpu.make_async_copy(source, target.at[spot], sems.at[n]))
    return copies


def stream(attn_plan, plan, seqs, scal, attn_refs, out_refs, heads, weights, attn_sems, sems):
    i = pl.program_id(0)
    seq, branch = scal[0], scal[1]
    cols = weights.shape[2]

    def place(js, jb):
        return (branch ^ jb) * seqs + (seq ^ js)

    def copies_of(k):
        columns = pl.ds((k % 2) * cols, cols)
        return fetch(plan[k // 2], out_refs, weights.at[k % 2], sems.at[k % 2], place, 0, columns)

    @pl.when(i == 0)
    def _():
        copies = fetch(attn_plan, attn_refs, heads, attn_sems, place, 1)
        for copy in copies + copies_of(0):
            copy.start()
        for copy in copies:
            copy.wait()

    steps = 2 * len(plan)
    for k in range(steps):

        @pl.when(i == k)
        def _():
            if k + 1 < steps:
                for copy in copies_of(k + 1):
                    copy.start()
            for copy in copies_of(k):
                copy.wait()

    return i % 2


def row_blocks(rows):
    block = min(128, rows)
    return [slice(start, start + block) for start in range(0, rows, block)]


def post_kernel(attn_plan, plan, seqs, n_attn, n_out, resume, scal, noise_ref, *refs):
    attn_refs, refs = refs[:n_attn], refs[n_attn:]
    out_refs, refs = refs[:n_out], refs[n_out:]
    noisy_ref, target_ref, shift_ref = refs[:3]
    refs = refs[3:]
    if resume:
        before_ref, refs = refs[0], refs[1:]
    term_ref, part_ref, refs = refs[0], refs[1], refs[2:]
    shares = refs[:seqs] if resume else ()
    grad_ref, heads, weights, cotangents, attn_sems, sems = refs[len(shares) :]
    slot = stream(
        attn_plan, plan, seqs, scal, attn_refs, out_refs, heads, weights, attn_sems, sems
    )

    @pl.when(pl.program_id(0) == 0)
    def _():
        grad_ref[...] = before_ref[...] if resume else jnp.zeros_like(grad_ref)

    noise = noise_ref[0]
    own_size = part_ref.shape[1]
    own = pl.ds(pl.multiple_of(scal[1] * own_size, own_size), own_size)
    for at in row_blocks(noisy_ref.shape[0]):
        term = dot(heads[at, :], weights[slot])
        term_ref[0, at, :] = term.astype(BF16)
        latent = noisy_ref[at, :].astype(F32)
        fake_pred = latent - noise * (latent + shift_ref[...] + term)
        cotangent = (noise * (-1.0 / 64.0)) * (fake_pred - target_ref[at, :].astype(F32))
        cotangents[at, :] = cotangent.astype(BF16)
        grad_ref[at, :] += contract(cotangents[at, :], weights[slot, own, :], 1, 1)
    part_ref[0] = contract(heads[:, own], cotangents[...], 0, 0).astype(BF16)
    if resume:

        @pl.when(pl.program_id(0) == pl.num_programs(0) - 1)
        def _():
            for d, share in enumerate(shares):
                head = share.shape[1]
                first = pl.multiple_of((scal[0] ^ d) * head, head)
                share[...] = grad_ref[:, pl.ds(first, head)].astype(BF16)


def plan_heads(plan):
    return len(plan[0])


def post(attn, out, blocks, scal, noise, noisy, target, shift, seqs, head, before):
    rows = target.shape[0]
    total = plan_heads(out.chunks)
    cols = out.operands[0].shape[-1] // 2
    chunks = len(out.chunks)
    n_attn, n_out = len(attn.operands), len(out.operands)
    kernel = functools.partial(
        post_kernel, attn.chunks[0], out.chunks, seqs, n_attn, n_out, len(before)
    )
    grad_spec = pl.BlockSpec((rows, seqs * head), lambda i, s: (0, 0))
    grad_specs, grad_shapes = [grad_spec], [jax.ShapeDtypeStruct((rows, seqs * head), F32)]
    scratch = []
    if before:
        grad_specs = [pl.BlockSpec((rows, head), lambda i, s: (0, 0))] * seqs
        grad_shapes = [jax.ShapeDtypeStruct((rows, head), BF16)] * seqs
        scratch = [pltpu.VMEM((rows, seqs * head), F32)]

    def spot(i, s):
        return s[2 + blocks + i // 2] * 2 + i % 2

    return pl.pallas_call(
        kernel,
        grid_spec=pltpu.PrefetchScalarGridSpec(
            num_scalar_prefetch=1,
            grid=(2 * chunks,),
            in_specs=[SMEM]
            + [ANY] * (n_attn + n_out)
            + [
                pl.BlockSpec((rows, cols), lambda i, s: (s[0], spot(i, s))),
                pl.BlockSpec((rows, cols), lambda i, s: (0, spot(i, s))),
                pl.BlockSpec((1, cols), lambda i, s: (0, spot(i, s))),
            ]
            + [grad_spec] * len(before),
            out_specs=[
                pl.BlockSpec((1, rows, cols), lambda i, s: (i // 2, 0, i % 2)),
                pl.BlockSpec((1, seqs * head, cols), lambda i, s: (i // 2, 0, i % 2)),
            ]
            + grad_specs,
            scratch_shapes=scratch
            + [
                pltpu.VMEM((rows, total * head), BF16),
                pltpu.VMEM((2, total * head, cols), BF16),
                pltpu.VMEM((rows, cols), BF16),
                pltpu.SemaphoreType.DMA((total,)),
                pltpu.SemaphoreType.DMA((2, total)),
            ],
        ),
        out_shape=[
            jax.ShapeDtypeStruct((chunks, rows, 2 * cols), BF16),
            jax.ShapeDtypeStruct((chunks, seqs * head, 2 * cols), BF16),
        ]
        + grad_shapes,
        cost_estimate=pl.CostEstimate(
            flops=4 * rows * chunks * cols * head * (total + 2 * seqs),
            bytes_accessed=2 * chunks * cols * (2 * total * head + 8 * rows),
            transcendentals=0,
        ),
    )(scal, noise, *attn.operands, *out.operands, noisy, target, shift, *before)


def guide_kernel(attn_plan, plan, seqs, n_attn, n_out, scal, noise_ref, *refs):
    attn_refs, refs = refs[:n_attn], refs[n_attn:]
    out_refs, refs = refs[:n_out], refs[n_out:]
    noisy_ref, target_ref, cond_ref, null_ref, near_ref, far_ref, diff_ref, total_ref = refs[:8]
    sum_ref, heads, weights, attn_sems, sems = refs[8:]
    slot = stream(
        attn_plan, plan, seqs, scal, attn_refs, out_refs, heads, weights, attn_sems, sems
    )

    @pl.when(pl.program_id(0) == 0)
    def _():
        sum_ref[...] = jnp.zeros_like(sum_ref)

    noise = noise_ref[0]
    own = pl.program_id(0) < pl.num_programs(0) // 2
    cond = cond_ref[...]
    mixed = guidance * cond - (guidance - 1.0) * null_ref[...]
    for at in row_blocks(noisy_ref.shape[0]):
        guided = dot(heads[at, :], weights[slot]) + mixed
        latent = noisy_ref[at, :].astype(F32)
        real_pred = latent - noise * (latent + guided)
        distance = jnp.abs(real_pred - target_ref[at, :].astype(F32))
        sum_ref[...] += jnp.sum(distance.reshape(-1, 8, distance.shape[1]), axis=0)
        term = jnp.where(own, near_ref[0, at, :].astype(F32), far_ref[0, at, :].astype(F32))
        diff_ref[at, :] = (noise * (guided - (cond + term))).astype(BF16)

    @pl.when(pl.program_id(0) == pl.num_programs(0) - 1)
    def _():
        total_ref[...] = jnp.broadcast_to(jnp.sum(sum_ref[...]), total_ref.shape)


def guide(attn, out, scal, noise, noisy, target, cond, null, near, far, seqs, head):
    rows, width = target.shape
    total = plan_heads(out.chunks)
    cols = out.operands[0].shape[-1] // 2
    chunks = len(out.chunks)
    n_attn, n_out = len(attn.operands), len(out.operands)

    def spot(i, s):
        return s[2 + i // 2] * 2 + i % 2

    column = pl.BlockSpec((1, cols), lambda i, s: (0, spot(i, s)))
    last = chunks - 1

    def near_spot(i, s):
        return (jnp.minimum(i, last) // 2, 0, jnp.minimum(i, last) % 2)

    def far_spot(i, s):
        return (jnp.maximum(i - last - 1, 0) // 2, 0, jnp.maximum(i - last - 1, 0) % 2)

    return pl.pallas_call(
        functools.partial(guide_kernel, attn.chunks[0], out.chunks, seqs, n_attn, n_out),
        grid_spec=pltpu.PrefetchScalarGridSpec(
            num_scalar_prefetch=1,
            grid=(2 * chunks,),
            in_specs=[SMEM]
            + [ANY] * (n_attn + n_out)
            + [
                pl.BlockSpec((rows, cols), lambda i, s: (s[0], spot(i, s))),
                pl.BlockSpec((rows, cols), lambda i, s: (0, spot(i, s))),
                column,
                column,
                pl.BlockSpec((1, rows, cols), near_spot),
                pl.BlockSpec((1, rows, cols), far_spot),
            ],
            out_specs=[
                pl.BlockSpec((rows, cols), lambda i, s: (0, spot(i, s))),
                pl.BlockSpec((8, 128), lambda i, s: (0, 0)),
            ],
            scratch_shapes=[
                pltpu.VMEM((8, cols), F32),
                pltpu.VMEM((rows, total * head), BF16),
                pltpu.VMEM((2, total * head, cols), BF16),
                pltpu.SemaphoreType.DMA((total,)),
                pltpu.SemaphoreType.DMA((2, total)),
            ],
        ),
        out_shape=[jax.ShapeDtypeStruct((rows, width), BF16), jax.ShapeDtypeStruct((8, 128), F32)],
        cost_estimate=pl.CostEstimate(
            flops=2 * rows * width * head * total,
            bytes_accessed=width * (2 * total * head + 8 * rows),
            transcendentals=0,
        ),
        compiler_params=GRANT,
    )(scal, noise, *attn.operands, *out.operands, noisy, target, cond, null, near, far)


def backward_kernel(
    seqs, per, scal, q_ref, k_ref, v_ref, qkv_ref, gain_ref, cos_ref, sin_ref, *refs
):
    shares = refs[:seqs]
    out_ref, grad_rows, key_sum, value_sum = refs[seqs:]
    tile, head = q_ref.shape
    scale = head ** (-0.5)
    i = pl.program_id(0)
    at = pl.ds(pl.multiple_of(i * tile, tile), tile)

    @pl.when(i == 0)
    def _():
        key_sum[...] = jnp.zeros_like(key_sum)
        value_sum[...] = jnp.zeros_like(value_sum)

    def unroll(raw, grad_rot, gain, cosine, sine):
        grad_normed = grad_rot * cosine + rotate_back(grad_rot * sine)
        inverse = lax.rsqrt(jnp.mean(raw * raw, axis=-1, keepdims=True) + norm_eps)
        scaled = gain * grad_normed
        mean = jnp.mean(scaled * raw, axis=-1, keepdims=True)
        return inverse * scaled - raw * inverse * inverse * inverse * mean

    for d, share in enumerate(shares):

        @pl.when(i // per == (scal[0] ^ d))
        def _():
            grad_rows[...] = share[...]

    probability = softmax_rows(q_ref[...], k_ref[...], scale)
    grad_prob = contract(grad_rows[...], v_ref[...], 1, 1)
    inner = jnp.sum(grad_prob * probability, axis=-1, keepdims=True)
    grad_score = (probability * (grad_prob - inner) * scale).astype(BF16)
    grad_query = unroll(
        qkv_ref[0, at, :head],
        dot(grad_score, k_ref[...]),
        gain_ref[0:1, :],
        cos_ref[at, :],
        sin_ref[at, :],
    )
    out_ref[:head, at] = grad_query.T.astype(BF16)
    key_sum[...] += contract(grad_score, q_ref[...], 0, 0)
    value_sum[...] += contract(probability.astype(BF16), grad_rows[...], 0, 0)

    @pl.when(i == pl.num_programs(0) - 1)
    def _():
        grad_key = unroll(
            qkv_ref[0, :, head : 2 * head],
            key_sum[...],
            gain_ref[1:2, :],
            cos_ref[...],
            sin_ref[...],
        )
        out_ref[head : 2 * head, :] = grad_key.T.astype(BF16)
        out_ref[2 * head :, :] = value_sum[...].T.astype(BF16)


def backward(scal, query, key, value, grad_attn, qkv, gains, cosine, sine):
    length, head = query.shape
    seqs = len(grad_attn)
    rows = length // seqs
    tile = min(256, rows)
    per = rows // tile
    row = pl.BlockSpec((tile, head), lambda i, s: (i, 0))

    def share(d):
        return pl.BlockSpec(
            (tile, head), lambda i, s: (jnp.clip(i - (s[0] ^ d) * per, 0, per - 1), 0)
        )

    return pl.pallas_call(
        functools.partial(backward_kernel, seqs, per),
        grid_spec=pltpu.PrefetchScalarGridSpec(
            num_scalar_prefetch=1,
            grid=(length // tile,),
            in_specs=[
                row,
                resident((length, head)),
                resident((length, head)),
                resident(qkv.shape),
                resident(gains.shape),
                resident(cosine.shape),
                resident(sine.shape),
            ]
            + [share(d) for d in range(seqs)],
            out_specs=pl.BlockSpec((3 * head, length), lambda i, s: (0, 0)),
            scratch_shapes=[
                pltpu.VMEM((tile, head), BF16),
                pltpu.VMEM((length, head), F32),
                pltpu.VMEM((length, head), F32),
            ],
        ),
        out_shape=jax.ShapeDtypeStruct((3 * head, length), BF16),
        cost_estimate=pl.CostEstimate(
            flops=20 * length * length * head,
            bytes_accessed=12 * length * head,
            transcendentals=length * length,
        ),
    )(scal, query, key, value, qkv, gains, cosine, sine, *grad_attn)


def weight_kernel(scal, grad_ref, hidden_ref, out_ref):
    out_ref[0] = dot(grad_ref[...], hidden_ref[...]).astype(BF16)


def weight_grad(grads, hidden, blocks, count, scal, cols):
    features, length = grads.shape
    parts = 2
    tile = cols // parts
    return pl.pallas_call(
        weight_kernel,
        grid_spec=pltpu.PrefetchScalarGridSpec(
            num_scalar_prefetch=1,
            grid=(count, parts),
            in_specs=[
                pl.BlockSpec((features, length), lambda i, p, s: (0, 0)),
                pl.BlockSpec((length, tile), lambda i, p, s: (0, s[2 + blocks + i] * parts + p)),
            ],
            out_specs=pl.BlockSpec((1, features, tile), lambda i, p, s: (i, 0, p)),
        ),
        out_shape=jax.ShapeDtypeStruct((count, features, cols), BF16),
        cost_estimate=pl.CostEstimate(
            flops=2 * count * cols * features * length,
            bytes_accessed=2 * count * cols * (length + features),
            transcendentals=0,
        ),
    )(scal, grads, hidden)


def spread_heads(value, axis, order, which):
    held, orders = [value], list(order)
    for d in range(1, lax.axis_size(axis)):
        held.append(move(value, axis, d))
        orders += [(js ^ d, jb) if which == 0 else (js, jb ^ d) for js, jb in order]
    return held, orders


def scale_kernel(entries, *refs):
    diff_ref, out_ref = refs[-2:]
    total = sum(ref[0:1, 0:1] for ref in refs[:-2])
    inverse = 1.0 / (total / entries + 1e-05)
    out_ref[...] = (diff_ref[...].astype(F32) * inverse).astype(BF16)


def scale(diff, totals, entries):
    rows, width = diff.shape
    tile = min(64, rows)
    block = pl.BlockSpec((tile, width), lambda i: (i, 0))
    return pl.pallas_call(
        functools.partial(scale_kernel, entries),
        grid=(rows // tile,),
        in_specs=[resident(totals[0].shape)] * len(totals) + [block],
        out_specs=block,
        out_shape=jax.ShapeDtypeStruct((rows, width), BF16),
        cost_estimate=pl.CostEstimate(
            flops=4 * rows * width, bytes_accessed=4 * rows * width, transcendentals=0
        ),
        compiler_params=GRANT,
    )(*totals, diff)


def turn_kernel(*refs):
    terms, out_ref = refs[:-1], refs[-1]
    head = out_ref.shape[2]
    for k in range(3):
        at = slice(k * head, (k + 1) * head)
        value = sum(term[0, at, :].astype(F32) for term in terms)
        out_ref[k] = value.T


def turn(terms, head):
    features, cols = terms[0].shape[1:]
    tile = cols // 2
    return pl.pallas_call(
        turn_kernel,
        grid=(cols // tile,),
        in_specs=[pl.BlockSpec((1, features, tile), lambda i: (0, 0, i))] * len(terms),
        out_specs=pl.BlockSpec((3, tile, head), lambda i: (0, i, 0)),
        out_shape=jax.ShapeDtypeStruct((3, cols, head), F32),
        cost_estimate=pl.CostEstimate(
            flops=3 * features * cols, bytes_accessed=10 * features * cols, transcendentals=0
        ),
        compiler_params=GRANT,
    )(*terms)


def gather_out(weight, rep):
    size = lax.axis_size("rep")
    cols = weight.shape[1] // size
    far = [bit for bit in bits_of(size) if bit > 1]
    mine = lax.dynamic_slice_in_dim(weight, rep * cols, cols, 1)[None]
    held, order = spread_heads(mine, "branch", [(0, 0)], 1)
    middle = max(len(held) // 2, 1)
    near_plan, far_plan = Plan(), Plan()
    near_plan.chunks = [[] for _ in range(size // 2)]
    far_plan.chunks = [[] for _ in range(size // 2)]

    def add(value, heads):
        for plan, v in ((near_plan, value), (far_plan, move(value, "rep", 1))):
            op = plan.add(v)
            for chunk, lead, js, jb in heads:
                plan.chunks[chunk].append((op, lead, js, jb))

    value = jnp.concatenate(held[:middle], axis=0)
    others, heads = spread_heads(value, "seq", order[:middle], 0)
    pieces = [jnp.concatenate(others, axis=0)]
    for bit in far:
        pieces += [move(piece, "rep", bit) for piece in pieces]
    for q, piece in enumerate(pieces):
        add(piece, [(q, (n,), js, jb) for n, (js, jb) in enumerate(heads)])

    value = jnp.concatenate(held[middle:], axis=0)[None]
    for bit in far:
        value = jnp.concatenate([value, move(value, "rep", bit)], axis=0)
    seqs = lax.axis_size("seq")
    for d in range(seqs):
        piece = move(value, "seq", d) if d else value
        heads = [
            (q, (q, n), d, jb)
            for q in range(value.shape[0])
            for n, (_, jb) in enumerate(order[middle:])
        ]
        add(piece, heads)
    return near_plan, far_plan


def gather_heads(attended):
    seqs = len(attended)
    held = [attended[0]] + [move(attended[d], "seq", d) for d in range(1, seqs)]
    held, order = spread_heads(jnp.stack(held), "branch", [(d, 0) for d in range(seqs)], 1)
    plan = Plan()
    chunk = []
    for n, (js, jb) in enumerate(order):
        if n % seqs == 0:
            op = plan.add(held[n // seqs])
        chunk.append((op, (n % seqs,), js, jb))
    plan.chunks.append(chunk)
    return plan


def body(
    noisy,
    generated,
    caption,
    null_caption,
    caption_drop,
    timestep,
    window_start,
    teacher_qkv,
    teacher_out,
    teacher_gain,
    teacher_qk_gain,
    critic_qkv,
    critic_out,
    critic_gain,
    critic_qk_gain,
):
    length, width = noisy.shape[1:]
    head = critic_out.shape[0]
    seqs, reps = lax.axis_size("seq"), lax.axis_size("rep")
    seq, rep, branch = lax.axis_index("seq"), lax.axis_index("rep"), lax.axis_index("branch")
    cols = width // reps
    fraction = (timestep.astype(F32) + 1.0) / 1001.0
    noise = 5.0 * fraction / (1.0 + 4.0 * fraction)
    used_caption = jnp.where(caption_drop[0] == 1, null_caption, caption[0])
    cond_shift = used_caption.astype(F32)[None, :]
    null_shift = null_caption.astype(F32)[None, :]
    both_shift = jnp.concatenate([cond_shift, null_shift], axis=0)
    latent = noisy[0]
    target = generated[0]
    far = [bit for bit in bits_of(reps) if bit > 1]
    chunks = [0]
    for bit in far:
        chunks += [j ^ bit for j in chunks]
    kept = len(chunks)
    chunks += [j ^ 1 for j in chunks]
    scal = jnp.stack([seq, branch] + [rep ^ j for j in chunks]).astype(jnp.int32)

    critic_near, critic_far = gather_out(critic_out, rep)
    cosine, sine = rope_tables(window_start[0], length)
    fake_qkv, hidden = project(latent, cond_shift, critic_gain[None], critic_qkv, True, 0, length)
    later, fake_qkv = lax.optimization_barrier((rep, fake_qkv))
    fake_attn, (fake_q, fake_k, fake_v) = attend(
        scal, seqs, fake_qkv, critic_qk_gain, cosine, sine, True
    )
    fake_plan = gather_heads(fake_attn)
    teacher_near, teacher_far = gather_out(teacher_out, later)
    half = length // 2
    both_qkv = ()
    for start in (0, half):
        both_qkv = project(
            latent, both_shift, teacher_gain[None], teacher_qkv, False, start, half, into=both_qkv
        )
    (both_qkv,) = both_qkv
    guided_attn, _ = attend(scal, seqs, both_qkv, teacher_qk_gain, cosine, sine, False)
    guided_plan = gather_heads(guided_attn)

    common = (noise, latent, target, cond_shift, seqs, head)
    near_term, near_part, near_grad = post(fake_plan, critic_near, 0, scal, *common, ())
    far_term, far_part, *grad_heads = post(fake_plan, critic_far, kept, scal, *common, (near_grad,))

    grad_attn = [grad_heads[0]]
    grad_attn += [move(grad_heads[d], "seq", d) for d in range(1, seqs)]

    grads = backward(
        scal, fake_q, fake_k, fake_v, grad_attn, fake_qkv, critic_qk_gain, cosine, sine
    )
    far_weight = weight_grad(grads, hidden, kept, kept, scal, cols)
    near_weight = weight_grad(grads, hidden, 0, kept, scal, cols)

    def reduce_rep(kept_part, sent_part):
        terms = [kept_part, move(sent_part, "rep", 1)]
        for bit in far[::-1]:
            split = bit // 2
            upper = sum(term[split : 2 * split].astype(F32) for term in terms).astype(BF16)
            terms = terms + [move(upper, "rep", bit)]
        return terms

    terms = reduce_rep(near_part, far_part)

    def out_block(d):
        return sum(
            lax.dynamic_slice(term, (0, (seq ^ d) * head, 0), (1, head, cols))[0].astype(F32)
            for term in terms
        )

    out_grad = out_block(0)
    for d in range(1, seqs):
        out_grad += move(out_block(d).astype(BF16), "seq", d).astype(F32)

    proj_terms = reduce_rep(near_weight, far_weight)
    proj_grad = turn(proj_terms, head)

    teacher_plan = Plan()
    shift_ops = len(teacher_near.operands)
    teacher_plan.operands = teacher_near.operands + teacher_far.operands
    teacher_plan.chunks = teacher_near.chunks + [
        [(op + shift_ops, lead, js, jb) for op, lead, js, jb in chunk]
        for chunk in teacher_far.chunks
    ]
    diff, partial = guide(
        guided_plan,
        teacher_plan,
        scal,
        noise,
        latent,
        target,
        cond_shift,
        null_shift,
        near_term,
        far_term,
        seqs,
        head,
    )
    totals = [partial] + [move(partial, "seq", d) for d in range(1, seqs)]
    result = scale(diff, totals, length * width)
    return result[None], proj_grad, out_grad


def solution(mesh):
    in_specs = (
        P("rep", None, None),
        P("rep", "seq", None),
        P("rep", None),
        P(),
        P("rep"),
        P("rep"),
        P("rep"),
        P(None, None, ("branch", "seq")),
        P(("branch", "seq"), None),
        P(),
        P(None, ("branch", "seq")),
        P(None, None, ("branch", "seq")),
        P(("branch", "seq"), None),
        P(),
        P(None, ("branch", "seq")),
    )
    out_specs = (
        P("rep", "seq", None),
        P(None, "rep", ("branch", "seq")),
        P(("branch", "seq"), "rep"),
    )
    return jax.shard_map(
        body,
        mesh=mesh,
        in_specs=in_specs,
        out_specs=out_specs,
        check_vma=False,
    )
```

```python
import functools
import jax
import jax.numpy as jnp
from jax import lax
from jax.experimental import pallas as pl
from jax.experimental.pallas import tpu as pltpu
from jax.sharding import PartitionSpec as P

GRID_H = 30
GRID_W = 52

guidance = 5.0
norm_eps = 1e-06

ANY = pl.BlockSpec(memory_space=pl.ANY)
SMEM = pl.BlockSpec(memory_space=pltpu.SMEM)
F32, BF16 = jnp.float32, jnp.bfloat16
GRANT = pltpu.CompilerParams(vmem_limit_bytes=32 << 20)


def swap(size, bit):
    return [(i, i ^ bit) for i in range(size)]


def bits_of(size):
    return [1 << k for k in range(size.bit_length() - 1)]


def move(value, axis, bit):
    return lax.ppermute(value, axis, swap(lax.axis_size(axis), bit))


def rope_tables(first_token, length):
    token_index = first_token + jnp.arange(length, dtype=jnp.int32)
    plane_size = GRID_H * GRID_W
    frame_index = token_index // plane_size
    remainder = token_index - frame_index * plane_size
    row_index = remainder // GRID_W
    column_index = remainder - row_index * GRID_W
    pair_index = jnp.arange(64, dtype=jnp.int32)
    in_frames = pair_index < 22
    in_rows = jnp.logical_and(pair_index >= 22, pair_index < 43)
    local_rank = jnp.where(
        in_frames, pair_index, jnp.where(in_rows, pair_index - 22, pair_index - 43)
    ).astype(jnp.float32)
    axis_width = jnp.where(in_frames, 44.0, 42.0).astype(jnp.float32)
    frequency = jnp.exp(-jnp.log(10000.0) * 2.0 * local_rank / axis_width)
    chosen = jnp.where(
        in_frames[None, :],
        frame_index[:, None],
        jnp.where(in_rows[None, :], row_index[:, None], column_index[:, None]),
    ).astype(jnp.float32)
    angles = chosen * frequency[None, :]
    angles = jnp.concatenate([angles, angles], axis=1)
    return (jnp.cos(angles), jnp.sin(angles))


def dot(left, right):
    return jnp.dot(left, right, preferred_element_type=F32)


def contract(left, right, left_dim, right_dim):
    return lax.dot_general(
        left, right, (((left_dim,), (right_dim,)), ((), ())), preferred_element_type=F32
    )


def rotate_half(values):
    half = values.shape[-1] // 2
    return jnp.concatenate([-values[..., half:], values[..., :half]], axis=-1)


def rotate_back(values):
    half = values.shape[-1] // 2
    return jnp.concatenate([values[..., half:], -values[..., :half]], axis=-1)


def resident(shape):
    return pl.BlockSpec(shape, lambda *_: (0,) * len(shape), pipeline_mode=pl.Buffered(1))


def project_kernel(variants, keep, held, noisy_ref, shift_ref, gain_ref, weight_ref, *refs):
    refs = refs[held:]
    out_ref = refs[0]
    hidden_ref = refs[1] if keep else None
    joined, normed, sems = refs[-3:]
    tile, width = noisy_ref.shape
    head = weight_ref.shape[2]
    copies = [
        pltpu.make_async_copy(
            weight_ref.at[k], joined.at[:, pl.ds(k * head, head)], sems.at[k]
        )
        for k in range(3)
    ]

    @pl.when(pl.program_id(0) == 0)
    def _():
        for copy in copies:
            copy.start()

    def step(t, carry):
        for u in range(2):
            at = pl.ds(pl.multiple_of(t * 32 + u * 16, 16), 16)
            latent = noisy_ref[at, :].astype(F32)
            for v in range(variants):
                shifted = latent + shift_ref[v : v + 1, :]
                mean = jnp.sum(shifted * shifted, axis=-1, keepdims=True) / width
                scaled = shifted * lax.rsqrt(mean + norm_eps) * gain_ref[...]
                normed[v, at, :] = scaled.astype(BF16)
        return carry

    lax.fori_loop(0, tile // 32, step, 0)

    @pl.when(pl.program_id(0) == 0)
    def _():
        for copy in copies:
            copy.wait()

    for v in range(variants):
        out_ref[v] = dot(normed[v], joined[...])
    if keep:
        hidden_ref[...] = normed[0]


def project(noisy, shifts, gain, weight, keep, start, count, into=()):
    length, width = noisy.shape
    head = weight.shape[2]
    variants = shifts.shape[0]
    tile = min(256, count)
    first = start // tile
    out_shape = [jax.ShapeDtypeStruct((variants, length, 3 * head), F32)]
    out_specs = [pl.BlockSpec((variants, tile, 3 * head), lambda i: (0, first + i, 0))]
    if keep:
        out_shape.append(jax.ShapeDtypeStruct((length, width), BF16))
        out_specs.append(pl.BlockSpec((tile, width), lambda i: (first + i, 0)))
    return pl.pallas_call(
        functools.partial(project_kernel, variants, keep, len(into)),
        grid=(count // tile,),
        in_specs=[
            pl.BlockSpec((tile, width), lambda i: (first + i, 0)),
            resident((variants, width)),
            resident((1, width)),
            ANY,
        ]
        + [ANY] * len(into),
        out_specs=out_specs,
        out_shape=out_shape,
        input_output_aliases={4 + n: n for n in range(len(into))},
        scratch_shapes=[
            pltpu.VMEM((width, 3 * head), BF16),
            pltpu.VMEM((variants, tile, width), BF16),
            pltpu.SemaphoreType.DMA((3,)),
        ],
        cost_estimate=pl.CostEstimate(
            flops=2 * variants * count * width * 3 * head,
            bytes_accessed=2 * count * width * (2 if keep else 1) + 6 * width * head,
            transcendentals=0,
        ),
    )(noisy, shifts, gain, weight, *into)


def rope_rows(raw, gain, cosine, sine):
    inverse = lax.rsqrt(jnp.mean(raw * raw, axis=-1, keepdims=True) + norm_eps)
    normed = raw * inverse * gain
    return (normed * cosine + rotate_half(normed) * sine).astype(BF16)


def softmax_rows(query, key, scale):
    exponent = jnp.exp(contract(query, key, 1, 1) * scale)
    return exponent / jnp.sum(exponent, axis=-1, keepdims=True)


def attend_kernel(variants, seqs, per, scal, qkv_ref, gain_ref, cos_ref, sin_ref, *refs):
    shares, saves = refs[:seqs], refs[seqs:-2]
    keys, values = refs[-2:]
    tile, head = shares[0].shape
    scale = head ** (-0.5)
    i = pl.program_id(0)

    @pl.when(i == 0)
    def _():
        for v in range(variants):
            keys[v] = rope_rows(
                qkv_ref[v, :, head : 2 * head], gain_ref[1:2, :], cos_ref[...], sin_ref[...]
            )
            values[v] = qkv_ref[v, :, 2 * head :].astype(BF16)
        if saves:
            saves[1][...] = keys[0]
            saves[2][...] = values[0]

    at = pl.ds(pl.multiple_of(i * tile, tile), tile)
    results = []
    for v in range(variants):
        query = rope_rows(qkv_ref[v, at, :head], gain_ref[0:1, :], cos_ref[at, :], sin_ref[at, :])
        if saves:
            saves[0][...] = query
        prob = softmax_rows(query, keys[v], scale).astype(BF16)
        results.append(dot(prob, values[v]).astype(BF16))
    result = results[0]
    if variants > 1:
        guided = guidance * results[0].astype(F32) - (guidance - 1.0) * results[1].astype(F32)
        result = guided.astype(BF16)
    for d, share in enumerate(shares):

        @pl.when(i // per == (scal[0] ^ d))
        def _():
            share[...] = result


def attend(scal, seqs, qkv, gains, cosine, sine, keep):
    variants, length, triple = qkv.shape
    head = triple // 3
    rows = length // seqs
    tile = min(256, rows)
    per = rows // tile
    saved = 3 if keep else 0
    row = pl.BlockSpec((tile, head), lambda i, s: (i, 0))
    whole = pl.BlockSpec((length, head), lambda i, s: (0, 0))
    flat = jax.ShapeDtypeStruct((length, head), BF16)

    def share(d):
        return pl.BlockSpec(
            (tile, head), lambda i, s: (jnp.clip(i - (s[0] ^ d) * per, 0, per - 1), 0)
        )

    results = pl.pallas_call(
        functools.partial(attend_kernel, variants, seqs, per),
        grid_spec=pltpu.PrefetchScalarGridSpec(
            num_scalar_prefetch=1,
            grid=(length // tile,),
            in_specs=[
                resident(qkv.shape),
                resident(gains.shape),
                resident(cosine.shape),
                resident(sine.shape),
            ],
            out_specs=[share(d) for d in range(seqs)] + [row, whole, whole][:saved],
            scratch_shapes=[
                pltpu.VMEM((variants, length, head), BF16),
                pltpu.VMEM((variants, length, head), BF16),
            ],
        ),
        out_shape=[jax.ShapeDtypeStruct((rows, head), BF16)] * seqs + [flat] * saved,
        cost_estimate=pl.CostEstimate(
            flops=16 * variants * length * length * head,
            bytes_accessed=4 * variants * length * triple,
            transcendentals=variants * length * length,
        ),
    )(scal, qkv, gains, cosine, sine)
    return results[:seqs], results[seqs:]


class Plan:
    def __init__(self):
        self.operands = []
        self.chunks = []

    def add(self, array):
        self.operands.append(array)
        return len(self.operands) - 1


def fetch(chunk, refs, target, sems, place, along, columns=None):
    copies = []
    for n, (op, lead, js, jb) in enumerate(chunk):
        source = refs[op]
        for index in lead:
            source = source.at[index]
        if columns is not None:
            source = source.at[:, columns]
        head = source.shape[along]
        first = pl.multiple_of(place(js, jb) * head, head)
        spot = (pl.ds(first, head), slice(None)) if along == 0 else (slice(None), pl.ds(first, head))
        copies.append(pltpu.make_async_copy(source, target.at[spot], sems.at[n]))
    return copies


def stream(attn_plan, plan, seqs, scal, attn_refs, out_refs, heads, weights, attn_sems, sems):
    i = pl.program_id(0)
    seq, branch = scal[0], scal[1]
    cols = weights.shape[2]

    def place(js, jb):
        return (branch ^ jb) * seqs + (seq ^ js)

    def copies_of(k):
        columns = pl.ds((k % 2) * cols, cols)
        return fetch(plan[k // 2], out_refs, weights.at[k % 2], sems.at[k % 2], place, 0, columns)

    @pl.when(i == 0)
    def _():
        copies = fetch(attn_plan, attn_refs, heads, attn_sems, place, 1)
        for copy in copies + copies_of(0):
            copy.start()
        for copy in copies:
            copy.wait()

    steps = 2 * len(plan)
    for k in range(steps):

        @pl.when(i == k)
        def _():
            if k + 1 < steps:
                for copy in copies_of(k + 1):
                    copy.start()
            for copy in copies_of(k):
                copy.wait()

    return i % 2


def row_blocks(rows):
    block = min(128, rows)
    return [slice(start, start + block) for start in range(0, rows, block)]


def post_kernel(attn_plan, plan, seqs, n_attn, n_out, resume, scal, noise_ref, *refs):
    attn_refs, refs = refs[:n_attn], refs[n_attn:]
    out_refs, refs = refs[:n_out], refs[n_out:]
    noisy_ref, target_ref, shift_ref = refs[:3]
    refs = refs[3:]
    if resume:
        before_ref, refs = refs[0], refs[1:]
    term_ref, part_ref, refs = refs[0], refs[1], refs[2:]
    shares = refs[:seqs] if resume else ()
    grad_ref, heads, weights, cotangents, attn_sems, sems = refs[len(shares) :]
    slot = stream(
        attn_plan, plan, seqs, scal, attn_refs, out_refs, heads, weights, attn_sems, sems
    )

    @pl.when(pl.program_id(0) == 0)
    def _():
        grad_ref[...] = before_ref[...] if resume else jnp.zeros_like(grad_ref)

    noise = noise_ref[0]
    own_size = part_ref.shape[1]
    own = pl.ds(pl.multiple_of(scal[1] * own_size, own_size), own_size)
    for at in row_blocks(noisy_ref.shape[0]):
        term = dot(heads[at, :], weights[slot])
        term_ref[0, at, :] = term.astype(BF16)
        latent = noisy_ref[at, :].astype(F32)
        fake_pred = latent - noise * (latent + shift_ref[...] + term)
        cotangent = (noise * (-1.0 / 64.0)) * (fake_pred - target_ref[at, :].astype(F32))
        cotangents[at, :] = cotangent.astype(BF16)
        grad_ref[at, :] += contract(cotangents[at, :], weights[slot, own, :], 1, 1)
    part_ref[0] = contract(heads[:, own], cotangents[...], 0, 0).astype(BF16)
    if resume:

        @pl.when(pl.program_id(0) == pl.num_programs(0) - 1)
        def _():
            for d, share in enumerate(shares):
                head = share.shape[1]
                first = pl.multiple_of((scal[0] ^ d) * head, head)
                share[...] = grad_ref[:, pl.ds(first, head)].astype(BF16)


def plan_heads(plan):
    return len(plan[0])


def post(attn, out, blocks, scal, noise, noisy, target, shift, seqs, head, before):
    rows = target.shape[0]
    total = plan_heads(out.chunks)
    cols = out.operands[0].shape[-1] // 2
    chunks = len(out.chunks)
    n_attn, n_out = len(attn.operands), len(out.operands)
    kernel = functools.partial(
        post_kernel, attn.chunks[0], out.chunks, seqs, n_attn, n_out, len(before)
    )
    grad_spec = pl.BlockSpec((rows, seqs * head), lambda i, s: (0, 0))
    grad_specs, grad_shapes = [grad_spec], [jax.ShapeDtypeStruct((rows, seqs * head), F32)]
    scratch = []
    if before:
        grad_specs = [pl.BlockSpec((rows, head), lambda i, s: (0, 0))] * seqs
        grad_shapes = [jax.ShapeDtypeStruct((rows, head), BF16)] * seqs
        scratch = [pltpu.VMEM((rows, seqs * head), F32)]

    def spot(i, s):
        return s[2 + blocks + i // 2] * 2 + i % 2

    return pl.pallas_call(
        kernel,
        grid_spec=pltpu.PrefetchScalarGridSpec(
            num_scalar_prefetch=1,
            grid=(2 * chunks,),
            in_specs=[SMEM]
            + [ANY] * (n_attn + n_out)
            + [
                pl.BlockSpec((rows, cols), lambda i, s: (s[0], spot(i, s))),
                pl.BlockSpec((rows, cols), lambda i, s: (0, spot(i, s))),
                pl.BlockSpec((1, cols), lambda i, s: (0, spot(i, s))),
            ]
            + [grad_spec] * len(before),
            out_specs=[
                pl.BlockSpec((1, rows, cols), lambda i, s: (i // 2, 0, i % 2)),
                pl.BlockSpec((1, seqs * head, cols), lambda i, s: (i // 2, 0, i % 2)),
            ]
            + grad_specs,
            scratch_shapes=scratch
            + [
                pltpu.VMEM((rows, total * head), BF16),
                pltpu.VMEM((2, total * head, cols), BF16),
                pltpu.VMEM((rows, cols), BF16),
                pltpu.SemaphoreType.DMA((total,)),
                pltpu.SemaphoreType.DMA((2, total)),
            ],
        ),
        out_shape=[
            jax.ShapeDtypeStruct((chunks, rows, 2 * cols), BF16),
            jax.ShapeDtypeStruct((chunks, seqs * head, 2 * cols), BF16),
        ]
        + grad_shapes,
        cost_estimate=pl.CostEstimate(
            flops=4 * rows * chunks * cols * head * (total + 2 * seqs),
            bytes_accessed=2 * chunks * cols * (2 * total * head + 8 * rows),
            transcendentals=0,
        ),
    )(scal, noise, *attn.operands, *out.operands, noisy, target, shift, *before)


def guide_kernel(attn_plan, plan, seqs, n_attn, n_out, scal, noise_ref, *refs):
    attn_refs, refs = refs[:n_attn], refs[n_attn:]
    out_refs, refs = refs[:n_out], refs[n_out:]
    noisy_ref, target_ref, cond_ref, null_ref, near_ref, far_ref, diff_ref, total_ref = refs[:8]
    sum_ref, heads, weights, attn_sems, sems = refs[8:]
    slot = stream(
        attn_plan, plan, seqs, scal, attn_refs, out_refs, heads, weights, attn_sems, sems
    )

    @pl.when(pl.program_id(0) == 0)
    def _():
        sum_ref[...] = jnp.zeros_like(sum_ref)

    noise = noise_ref[0]
    own = pl.program_id(0) < pl.num_programs(0) // 2
    cond = cond_ref[...]
    mixed = guidance * cond - (guidance - 1.0) * null_ref[...]
    for at in row_blocks(noisy_ref.shape[0]):
        guided = dot(heads[at, :], weights[slot]) + mixed
        latent = noisy_ref[at, :].astype(F32)
        real_pred = latent - noise * (latent + guided)
        distance = jnp.abs(real_pred - target_ref[at, :].astype(F32))
        sum_ref[...] += jnp.sum(distance.reshape(-1, 8, distance.shape[1]), axis=0)
        term = jnp.where(own, near_ref[0, at, :].astype(F32), far_ref[0, at, :].astype(F32))
        diff_ref[at, :] = (noise * (guided - (cond + term))).astype(BF16)

    @pl.when(pl.program_id(0) == pl.num_programs(0) - 1)
    def _():
        total_ref[...] = jnp.broadcast_to(jnp.sum(sum_ref[...]), total_ref.shape)


def guide(attn, out, scal, noise, noisy, target, cond, null, near, far, seqs, head):
    rows, width = target.shape
    total = plan_heads(out.chunks)
    cols = out.operands[0].shape[-1] // 2
    chunks = len(out.chunks)
    n_attn, n_out = len(attn.operands), len(out.operands)

    def spot(i, s):
        return s[2 + i // 2] * 2 + i % 2

    column = pl.BlockSpec((1, cols), lambda i, s: (0, spot(i, s)))
    last = chunks - 1

    def near_spot(i, s):
        return (jnp.minimum(i, last) // 2, 0, jnp.minimum(i, last) % 2)

    def far_spot(i, s):
        return (jnp.maximum(i - last - 1, 0) // 2, 0, jnp.maximum(i - last - 1, 0) % 2)

    return pl.pallas_call(
        functools.partial(guide_kernel, attn.chunks[0], out.chunks, seqs, n_attn, n_out),
        grid_spec=pltpu.PrefetchScalarGridSpec(
            num_scalar_prefetch=1,
            grid=(2 * chunks,),
            in_specs=[SMEM]
            + [ANY] * (n_attn + n_out)
            + [
                pl.BlockSpec((rows, cols), lambda i, s: (s[0], spot(i, s))),
                pl.BlockSpec((rows, cols), lambda i, s: (0, spot(i, s))),
                column,
                column,
                pl.BlockSpec((1, rows, cols), near_spot),
                pl.BlockSpec((1, rows, cols), far_spot),
            ],
            out_specs=[
                pl.BlockSpec((rows, cols), lambda i, s: (0, spot(i, s))),
                pl.BlockSpec((8, 128), lambda i, s: (0, 0)),
            ],
            scratch_shapes=[
                pltpu.VMEM((8, cols), F32),
                pltpu.VMEM((rows, total * head), BF16),
                pltpu.VMEM((2, total * head, cols), BF16),
                pltpu.SemaphoreType.DMA((total,)),
                pltpu.SemaphoreType.DMA((2, total)),
            ],
        ),
        out_shape=[jax.ShapeDtypeStruct((rows, width), BF16), jax.ShapeDtypeStruct((8, 128), F32)],
        cost_estimate=pl.CostEstimate(
            flops=2 * rows * width * head * total,
            bytes_accessed=width * (2 * total * head + 8 * rows),
            transcendentals=0,
        ),
        compiler_params=GRANT,
    )(scal, noise, *attn.operands, *out.operands, noisy, target, cond, null, near, far)


def backward_kernel(
    seqs, per, scal, q_ref, k_ref, v_ref, qkv_ref, gain_ref, cos_ref, sin_ref, *refs
):
    shares = refs[:seqs]
    out_ref, grad_rows, key_sum, value_sum = refs[seqs:]
    tile, head = q_ref.shape
    scale = head ** (-0.5)
    i = pl.program_id(0)
    at = pl.ds(pl.multiple_of(i * tile, tile), tile)

    @pl.when(i == 0)
    def _():
        key_sum[...] = jnp.zeros_like(key_sum)
        value_sum[...] = jnp.zeros_like(value_sum)

    def unroll(raw, grad_rot, gain, cosine, sine):
        grad_normed = grad_rot * cosine + rotate_back(grad_rot * sine)
        inverse = lax.rsqrt(jnp.mean(raw * raw, axis=-1, keepdims=True) + norm_eps)
        scaled = gain * grad_normed
        mean = jnp.mean(scaled * raw, axis=-1, keepdims=True)
        return inverse * scaled - raw * inverse * inverse * inverse * mean

    for d, share in enumerate(shares):

        @pl.when(i // per == (scal[0] ^ d))
        def _():
            grad_rows[...] = share[...]

    probability = softmax_rows(q_ref[...], k_ref[...], scale)
    grad_prob = contract(grad_rows[...], v_ref[...], 1, 1)
    inner = jnp.sum(grad_prob * probability, axis=-1, keepdims=True)
    grad_score = (probability * (grad_prob - inner) * scale).astype(BF16)
    grad_query = unroll(
        qkv_ref[0, at, :head],
        dot(grad_score, k_ref[...]),
        gain_ref[0:1, :],
        cos_ref[at, :],
        sin_ref[at, :],
    )
    out_ref[:head, at] = grad_query.T.astype(BF16)
    key_sum[...] += contract(grad_score, q_ref[...], 0, 0)
    value_sum[...] += contract(probability.astype(BF16), grad_rows[...], 0, 0)

    @pl.when(i == pl.num_programs(0) - 1)
    def _():
        grad_key = unroll(
            qkv_ref[0, :, head : 2 * head],
            key_sum[...],
            gain_ref[1:2, :],
            cos_ref[...],
            sin_ref[...],
        )
        out_ref[head : 2 * head, :] = grad_key.T.astype(BF16)
        out_ref[2 * head :, :] = value_sum[...].T.astype(BF16)


def backward(scal, query, key, value, grad_attn, qkv, gains, cosine, sine):
    length, head = query.shape
    seqs = len(grad_attn)
    rows = length // seqs
    tile = min(256, rows)
    per = rows // tile
    row = pl.BlockSpec((tile, head), lambda i, s: (i, 0))

    def share(d):
        return pl.BlockSpec(
            (tile, head), lambda i, s: (jnp.clip(i - (s[0] ^ d) * per, 0, per - 1), 0)
        )

    return pl.pallas_call(
        functools.partial(backward_kernel, seqs, per),
        grid_spec=pltpu.PrefetchScalarGridSpec(
            num_scalar_prefetch=1,
            grid=(length // tile,),
            in_specs=[
                row,
                resident((length, head)),
                resident((length, head)),
                resident(qkv.shape),
                resident(gains.shape),
                resident(cosine.shape),
                resident(sine.shape),
            ]
            + [share(d) for d in range(seqs)],
            out_specs=pl.BlockSpec((3 * head, length), lambda i, s: (0, 0)),
            scratch_shapes=[
                pltpu.VMEM((tile, head), BF16),
                pltpu.VMEM((length, head), F32),
                pltpu.VMEM((length, head), F32),
            ],
        ),
        out_shape=jax.ShapeDtypeStruct((3 * head, length), BF16),
        cost_estimate=pl.CostEstimate(
            flops=20 * length * length * head,
            bytes_accessed=12 * length * head,
            transcendentals=length * length,
        ),
    )(scal, query, key, value, qkv, gains, cosine, sine, *grad_attn)


def weight_kernel(scal, grad_ref, hidden_ref, out_ref):
    out_ref[0] = dot(grad_ref[...], hidden_ref[...]).astype(BF16)


def weight_grad(grads, hidden, blocks, count, scal, cols):
    features, length = grads.shape
    parts = 2
    tile = cols // parts
    return pl.pallas_call(
        weight_kernel,
        grid_spec=pltpu.PrefetchScalarGridSpec(
            num_scalar_prefetch=1,
            grid=(count, parts),
            in_specs=[
                pl.BlockSpec((features, length), lambda i, p, s: (0, 0)),
                pl.BlockSpec((length, tile), lambda i, p, s: (0, s[2 + blocks + i] * parts + p)),
            ],
            out_specs=pl.BlockSpec((1, features, tile), lambda i, p, s: (i, 0, p)),
        ),
        out_shape=jax.ShapeDtypeStruct((count, features, cols), BF16),
        cost_estimate=pl.CostEstimate(
            flops=2 * count * cols * features * length,
            bytes_accessed=2 * count * cols * (length + features),
            transcendentals=0,
        ),
    )(scal, grads, hidden)


def spread_heads(value, axis, order, which):
    held, orders = [value], list(order)
    for d in range(1, lax.axis_size(axis)):
        held.append(move(value, axis, d))
        orders += [(js ^ d, jb) if which == 0 else (js, jb ^ d) for js, jb in order]
    return held, orders


def scale_kernel(entries, *refs):
    diff_ref, out_ref = refs[-2:]
    total = sum(ref[0:1, 0:1] for ref in refs[:-2])
    inverse = 1.0 / (total / entries + 1e-05)
    out_ref[...] = (diff_ref[...].astype(F32) * inverse).astype(BF16)


def scale(diff, totals, entries):
    rows, width = diff.shape
    tile = min(64, rows)
    block = pl.BlockSpec((tile, width), lambda i: (i, 0))
    return pl.pallas_call(
        functools.partial(scale_kernel, entries),
        grid=(rows // tile,),
        in_specs=[resident(totals[0].shape)] * len(totals) + [block],
        out_specs=block,
        out_shape=jax.ShapeDtypeStruct((rows, width), BF16),
        cost_estimate=pl.CostEstimate(
            flops=4 * rows * width, bytes_accessed=4 * rows * width, transcendentals=0
        ),
        compiler_params=GRANT,
    )(*totals, diff)


def turn_kernel(*refs):
    terms, out_ref = refs[:-1], refs[-1]
    head = out_ref.shape[2]
    for k in range(3):
        at = slice(k * head, (k + 1) * head)
        value = sum(term[0, at, :].astype(F32) for term in terms)
        out_ref[k] = value.T


def turn(terms, head):
    features, cols = terms[0].shape[1:]
    tile = cols // 2
    return pl.pallas_call(
        turn_kernel,
        grid=(cols // tile,),
        in_specs=[pl.BlockSpec((1, features, tile), lambda i: (0, 0, i))] * len(terms),
        out_specs=pl.BlockSpec((3, tile, head), lambda i: (0, i, 0)),
        out_shape=jax.ShapeDtypeStruct((3, cols, head), F32),
        cost_estimate=pl.CostEstimate(
            flops=3 * features * cols, bytes_accessed=10 * features * cols, transcendentals=0
        ),
        compiler_params=GRANT,
    )(*terms)


def gather_out(weight, rep):
    size = lax.axis_size("rep")
    cols = weight.shape[1] // size
    far = [bit for bit in bits_of(size) if bit > 1]
    mine = lax.dynamic_slice_in_dim(weight, rep * cols, cols, 1)[None]
    held, order = spread_heads(mine, "branch", [(0, 0)], 1)
    middle = max(len(held) // 2, 1)
    near_plan, far_plan = Plan(), Plan()
    near_plan.chunks = [[] for _ in range(size // 2)]
    far_plan.chunks = [[] for _ in range(size // 2)]

    def add(value, heads):
        for plan, v in ((near_plan, value), (far_plan, move(value, "rep", 1))):
            op = plan.add(v)
            for chunk, lead, js, jb in heads:
                plan.chunks[chunk].append((op, lead, js, jb))

    value = jnp.concatenate(held[:middle], axis=0)
    others, heads = spread_heads(value, "seq", order[:middle], 0)
    pieces = [jnp.concatenate(others, axis=0)]
    for bit in far:
        pieces += [move(piece, "rep", bit) for piece in pieces]
    for q, piece in enumerate(pieces):
        add(piece, [(q, (n,), js, jb) for n, (js, jb) in enumerate(heads)])

    value = jnp.concatenate(held[middle:], axis=0)[None]
    for bit in far:
        value = jnp.concatenate([value, move(value, "rep", bit)], axis=0)
    seqs = lax.axis_size("seq")
    for d in range(seqs):
        piece = move(value, "seq", d) if d else value
        heads = [
            (q, (q, n), d, jb)
            for q in range(value.shape[0])
            for n, (_, jb) in enumerate(order[middle:])
        ]
        add(piece, heads)
    return near_plan, far_plan


def gather_heads(attended):
    seqs = len(attended)
    held = [attended[0]] + [move(attended[d], "seq", d) for d in range(1, seqs)]
    held, order = spread_heads(jnp.stack(held), "branch", [(d, 0) for d in range(seqs)], 1)
    plan = Plan()
    chunk = []
    for n, (js, jb) in enumerate(order):
        if n % seqs == 0:
            op = plan.add(held[n // seqs])
        chunk.append((op, (n % seqs,), js, jb))
    plan.chunks.append(chunk)
    return plan


def body(
    noisy,
    generated,
    caption,
    null_caption,
    caption_drop,
    timestep,
    window_start,
    teacher_qkv,
    teacher_out,
    teacher_gain,
    teacher_qk_gain,
    critic_qkv,
    critic_out,
    critic_gain,
    critic_qk_gain,
):
    length, width = noisy.shape[1:]
    head = critic_out.shape[0]
    seqs, reps = lax.axis_size("seq"), lax.axis_size("rep")
    seq, rep, branch = lax.axis_index("seq"), lax.axis_index("rep"), lax.axis_index("branch")
    cols = width // reps
    fraction = (timestep.astype(F32) + 1.0) / 1001.0
    noise = 5.0 * fraction / (1.0 + 4.0 * fraction)
    used_caption = jnp.where(caption_drop[0] == 1, null_caption, caption[0])
    cond_shift = used_caption.astype(F32)[None, :]
    null_shift = null_caption.astype(F32)[None, :]
    both_shift = jnp.concatenate([cond_shift, null_shift], axis=0)
    latent = noisy[0]
    target = generated[0]
    far = [bit for bit in bits_of(reps) if bit > 1]
    chunks = [0]
    for bit in far:
        chunks += [j ^ bit for j in chunks]
    kept = len(chunks)
    chunks += [j ^ 1 for j in chunks]
    scal = jnp.stack([seq, branch] + [rep ^ j for j in chunks]).astype(jnp.int32)

    critic_near, critic_far = gather_out(critic_out, rep)
    cosine, sine = rope_tables(window_start[0], length)
    fake_qkv, hidden = project(latent, cond_shift, critic_gain[None], critic_qkv, True, 0, length)
    later, fake_qkv = lax.optimization_barrier((rep, fake_qkv))
    fake_attn, (fake_q, fake_k, fake_v) = attend(
        scal, seqs, fake_qkv, critic_qk_gain, cosine, sine, True
    )
    fake_plan = gather_heads(fake_attn)
    teacher_near, teacher_far = gather_out(teacher_out, later)
    half = length // 2
    both_qkv = ()
    for start in (0, half):
        both_qkv = project(
            latent, both_shift, teacher_gain[None], teacher_qkv, False, start, half, into=both_qkv
        )
    (both_qkv,) = both_qkv
    guided_attn, _ = attend(scal, seqs, both_qkv, teacher_qk_gain, cosine, sine, False)
    guided_plan = gather_heads(guided_attn)

    common = (noise, latent, target, cond_shift, seqs, head)
    near_term, near_part, near_grad = post(fake_plan, critic_near, 0, scal, *common, ())
    far_term, far_part, *grad_heads = post(fake_plan, critic_far, kept, scal, *common, (near_grad,))

    grad_attn = [grad_heads[0]]
    grad_attn += [move(grad_heads[d], "seq", d) for d in range(1, seqs)]

    grads = backward(
        scal, fake_q, fake_k, fake_v, grad_attn, fake_qkv, critic_qk_gain, cosine, sine
    )
    far_weight = weight_grad(grads, hidden, kept, kept, scal, cols)
    near_weight = weight_grad(grads, hidden, 0, kept, scal, cols)

    def reduce_rep(kept_part, sent_part):
        terms = [kept_part, move(sent_part, "rep", 1)]
        for bit in far[::-1]:
            split = bit // 2
            upper = sum(term[split : 2 * split].astype(F32) for term in terms).astype(BF16)
            terms = terms + [move(upper, "rep", bit)]
        return terms

    terms = reduce_rep(near_part, far_part)

    def out_block(d):
        return sum(
            lax.dynamic_slice(term, (0, (seq ^ d) * head, 0), (1, head, cols))[0].astype(F32)
            for term in terms
        )

    out_grad = out_block(0)
    for d in range(1, seqs):
        out_grad += move(out_block(d).astype(BF16), "seq", d).astype(F32)

    proj_terms = reduce_rep(near_weight, far_weight)
    proj_grad = turn(proj_terms, head)

    teacher_plan = Plan()
    shift_ops = len(teacher_near.operands)
    teacher_plan.operands = teacher_near.operands + teacher_far.operands
    teacher_plan.chunks = teacher_near.chunks + [
        [(op + shift_ops, lead, js, jb) for op, lead, js, jb in chunk]
        for chunk in teacher_far.chunks
    ]
    diff, partial = guide(
        guided_plan,
        teacher_plan,
        scal,
        noise,
        latent,
        target,
        cond_shift,
        null_shift,
        near_term,
        far_term,
        seqs,
        head,
    )
    totals = [partial] + [move(partial, "seq", d) for d in range(1, seqs)]
    result = scale(diff, totals, length * width)
    return result[None], proj_grad, out_grad


def solution(mesh):
    in_specs = (
        P("rep", None, None),
        P("rep", "seq", None),
        P("rep", None),
        P(),
        P("rep"),
        P("rep"),
        P("rep"),
        P(None, None, ("branch", "seq")),
        P(("branch", "seq"), None),
        P(),
        P(None, ("branch", "seq")),
        P(None, None, ("branch", "seq")),
        P(("branch", "seq"), None),
        P(),
        P(None, ("branch", "seq")),
    )
    out_specs = (
        P("rep", "seq", None),
        P(None, "rep", ("branch", "seq")),
        P(("branch", "seq"), "rep"),
    )
    return jax.shard_map(
        body,
        mesh=mesh,
        in_specs=in_specs,
        out_specs=out_specs,
        check_vma=False,
    )
```
